256 devices in a mesh: dp: 4 (over y), tensor: 64 (over x, z, core).
Axes of the slice: x: 4, y: 4, z: 8, core: 2. Of those that a mesh axis runs over, the one named last changes fastest.
Arguments:
- tokens: bfloat16 [4, 8192, 1536], P('dp', 'tensor'), may hold values from -6 to 6
- attn_gain: float32 [1536], replicated, may hold values from 0.1 to 1.9
- qkv_weight: bfloat16 [1536, 2560], P(None, 'dp'), may hold values from -0.25 to 0.25
- out_weight: bfloat16 [1536, 1536], P('dp'), may hold values from -0.15625 to 0.15625
- prefix_cache: bfloat16 [4, 512, 2, 512], P('dp', 'tensor'), may hold values from -640 to 640
- lengths: int32 [4, 256], P('dp'), may hold values from 1 to 384, 8192 in all within a row
- ffn_gain: float32 [1536], replicated, may hold values from 0.1 to 1.9
- expert_ids: int32 [4, 8192, 8], P('dp', 'tensor'), may hold values from 0 to 31, all different within a row; in each aligned block of 128 rows (0 to 127, 128 to 255, ..., all dimensions but the last counted through in order) at most 40 rows name the same one
- gate_weights: float32 [4, 8192, 8], P('dp', 'tensor'), may hold values from 0.05 to 0.5
- expert_in: bfloat16 [64, 1536, 512], P('tensor'), may hold values from -0.15625 to 0.15625
- expert_out: bfloat16 [64, 256, 1536], P('tensor'), may hold values from -0.25 to 0.25
Outputs:
- hidden_state: bfloat16 [4, 8192, 1536], P('dp', 'tensor')
- mixed: bfloat16 [4, 8192, 1536], P('dp', 'tensor')
The draws below stay inside these ranges and needn't reach their ends.
Inputs may be any that keep to these rules, and one draw needn't show every extreme that they name: `lengths`: each group's 256 requests fill its 8192 suffix positions in order, and the longest holds exactly 384 tokens. `expert_ids`: each token names 8 different experts; among the 128 tokens of one device no expert is named more than 40 times, a bound that some block reaches.
All inputs are finite; a program needn't handle non-finite values.
Results may differ from the reference program's by a relative error of at most 0.014.
The reference program's roundings to bfloat16 on the way count: a program that leaves them out, or rounds other values in their place, can miss the bound.
Values may be sent and summed in bfloat16 or wider, within the bound.
No kernel may reach another device: no remote copies, remote signals or barrier semaphores. Data moves between devices by JAX's collectives and lax.ppermute only.
A program may use at most 128 MiB of HBM per device.

```python
import math
import jax
import jax.numpy as jnp
import numpy as np
from jax import lax

D = 1536
HEADS = 24
KV_HEADS = 8
HEAD_DIM = 64
FF = 512
EXPERTS = 32
TOPK = 8
TOK_DEV = 128
REACH = 3
GROUPS = 4
SUFFIX = 8192
PREFIX = 512
MOST = 384
NREQ = 256
CAP = 40
SPLIT = 2
UNITS = 64
UNIT_FF = 256
QKV_W = 2560


def draw_prefix_cache(key, part):
    shape = (GROUPS, PREFIX, 2, KV_HEADS * HEAD_DIM)
    return jnp.clip(jax.random.normal(key, shape, jnp.float32) * 1.75, -8.0, 8.0).astype(jnp.bfloat16)


def block_levels(rng, dims, cuts, smallest, high):
    def one(dim, parts):
        draws = jax.random.uniform(jax.random.fold_in(jax.random.fold_in(rng, 6), dim), (parts,), jnp.float32, smallest / len(cuts), high / len(cuts))
        return jnp.repeat(jnp.exp(draws), dims[dim] // parts).reshape((-1,) + (1,) * (len(dims) - dim - 1))

    loudness = one(*cuts[0])
    for cut in cuts[1:]:
        loudness = loudness * one(*cut)
    return loudness


def split_up(count, total, bound, skew):
    portions = [(1 << 20) // math.isqrt(rank ** skew) + 1 for rank in range(2, count + 1)]
    rest, holding = total - bound - (count - 1), [1] * (count - 1)
    while rest > 0:
        movable = [i for i in range(count - 1) if holding[i] < bound]
        mass, left = sum([portions[i] for i in movable]), rest
        for i in movable:
            more = min(bound - holding[i], max(1, left * portions[i] // mass), rest)
            holding[i] = holding[i] + more
            rest = rest - more
    return np.array([bound] + holding)


def ragged_sizes(key, number_of, total, most, slope):
    if number_of == 2:
        one = jax.random.randint(key, (), max(1, total - most), min(most, total - 1) + 1)
        return jnp.stack([one, total - one])
    tallies = jnp.asarray(split_up(number_of, total, most, slope), jnp.int32)
    pairs = (number_of - 1) // 2
    giver, sink = tallies[1:1 + 2 * pairs:2], tallies[2:2 + 2 * pairs:2]
    margin = jnp.minimum(giver - 1, most - sink)
    moved = jax.random.randint(jax.random.fold_in(key, 1), (pairs,), 0, 1 << 20) % (margin + 1)
    tallies = tallies.at[1:1 + 2 * pairs:2].set(giver - moved).at[2:2 + 2 * pairs:2].set(sink + moved)
    return tallies[jax.random.permutation(jax.random.fold_in(key, 2), number_of)]


def assign_block(key, own, number, rows, count, top, reach, lean):
    sequence = jax.random.permutation(key, count)
    crowded, ordinary = load_shares(count, rows * top, reach, lean, True), load_shares(count, rows * top, reach, lean, False)
    places = jnp.arange(count)

    def named(tallies, turn):
        used = int((tallies > 0).sum())
        fixed = max(1, used // 4)
        passed = fixed + (places - fixed + turn * (used - fixed)) % max(1, count - fixed)
        return jnp.zeros((count,), jnp.int32).at[sequence[jnp.where(places < fixed, places, passed)]].set(jnp.asarray(tallies, jnp.int32))

    tallies = jnp.where(number % 4 == 0, named(crowded, number // 4), named(ordinary, number - number // 4 - 1))
    mixed = jax.random.permutation(jax.random.fold_in(own, 3), count)
    donor, receiver = mixed[0:count // 2 * 2:2], mixed[1:count // 2 * 2:2]
    margin = jnp.minimum(tallies[donor] - 1, reach - tallies[receiver]) // 2
    margin = jnp.where((donor == sequence[0]) | (receiver == sequence[0]) | (tallies[receiver] == 0), 0, jnp.maximum(margin, 0))
    passed = jax.random.randint(jax.random.fold_in(own, 4), (count // 2,), 0, 1 << 20) % (margin + 1)
    tallies = tallies.at[donor].add(-passed).at[receiver].add(passed)
    members = jnp.searchsorted(jnp.cumsum(tallies), jnp.arange(rows * top), side="right").astype(jnp.int32)
    listing = members.reshape(top, rows).T
    listing = listing[jax.random.permutation(jax.random.fold_in(own, 1), rows)]
    turn = jax.random.randint(jax.random.fold_in(own, 2), (rows, 1), 0, top)
    return jnp.take_along_axis(listing, (jnp.arange(top)[None, :] + turn) % top, axis=1)


def load_shares(amount, total, most, slope, full):
    loads = [(1 << 20) // math.isqrt(rank ** slope) + 1 for rank in range(1, amount + 1)]
    largest = most if full else min(most, max(-(-total // amount), total * loads[0] // sum(loads)))
    least = 1 if total - largest >= amount - 1 else 0
    given, spare = [largest] + [least] * (amount - 1), total - largest - least * (amount - 1)
    while spare > 0:
        free = [i for i in range(1, amount) if given[i] < largest] or [i for i in range(1, amount) if given[i] < most]
        pool, remaining = sum([loads[i] for i in free]), spare
        for i in free:
            extra = min(most - given[i], max(1, remaining * loads[i] // pool), spare)
            given[i] = given[i] + extra
            spare = spare - extra
    return np.array(given)


def centred(rng, shape, deviation, most, pieces=(), kind=jnp.bfloat16):
    values = deviation * jax.random.normal(rng, shape, jnp.float32)
    if pieces:
        values = values * block_levels(rng, shape, pieces, -0.22, 0.18)
    return jnp.clip(values, -most, most).astype(kind)


def setup_inputs(seed: int = 0) -> dict:
    seeds = jax.random.split(jax.random.key(seed), 12)
    tokens = centred(seeds[0], (GROUPS, SUFFIX, D), 1.0, 6.0, ((0, 4), (1, 64)))
    attn_gain = jnp.clip(1.0 + 0.18 * jax.random.normal(seeds[1], (D,), jnp.float32), 0.1, 1.9)
    qkv_weight = centred(seeds[2], (D, QKV_W), (D // 3) ** -0.5, 0.25, ((1, 4),))
    out_weight = centred(seeds[3], (HEADS * HEAD_DIM, D), (HEADS * HEAD_DIM) ** -0.5, 0.15625, ((0, 4),))
    prefix_cache = draw_prefix_cache(jax.random.fold_in(seeds[11], 71), 0)
    lengths = jax.vmap(lambda own: ragged_sizes(own, NREQ, SUFFIX, MOST, 3))(jax.random.split(seeds[5], GROUPS)).reshape((GROUPS, NREQ)).astype(jnp.int32)
    ffn_gain = jnp.clip(1.0 + 0.18 * jax.random.normal(seeds[6], (D,), jnp.float32), 0.1, 1.9)
    expert_ids_keys = jax.random.split(jax.random.fold_in(seeds[7], 1), GROUPS * SUFFIX // TOK_DEV)
    expert_ids_turns = jax.random.permutation(jax.random.fold_in(seeds[7], 3), GROUPS * SUFFIX // TOK_DEV)
    expert_ids = jax.vmap(lambda own, number: assign_block(jax.random.fold_in(seeds[7], 2), own, number, TOK_DEV, EXPERTS, TOPK, CAP, 2))(expert_ids_keys, expert_ids_turns).reshape((GROUPS, SUFFIX, TOPK))
    gate_weights = jnp.clip(jnp.exp(math.log(0.5) - 2.3025851 * jax.random.uniform(seeds[8], (GROUPS, SUFFIX, TOPK), jnp.float32) ** block_levels(seeds[8], (GROUPS, SUFFIX, TOPK), ((0, 4), (1, 64)), -0.2, 0.2)), 0.05, 0.5)
    expert_in = centred(seeds[9], (UNITS, D, 2 * UNIT_FF), D ** -0.5, 0.15625, ((0, 64),))
    expert_out = centred(seeds[10], (UNITS, UNIT_FF, D), FF ** -0.5, 0.25, ((0, 64),))
    return {"tokens": tokens, "attn_gain": attn_gain, "qkv_weight": qkv_weight, "out_weight": out_weight, "prefix_cache": prefix_cache, "lengths": lengths, "ffn_gain": ffn_gain, "expert_ids": expert_ids, "gate_weights": gate_weights, "expert_in": expert_in, "expert_out": expert_out}


EPS = 1e-06
THETA = 10000.0

def rms_norm(x, gain):
    values = x.astype(jnp.float32)
    mean_sq = lax.optimization_barrier(jnp.mean(values * values, axis=-1, keepdims=True))
    return (values * lax.rsqrt(mean_sq + EPS) * gain.astype(jnp.float32)).astype(jnp.bfloat16)

def rotary(x, positions):
    half = x.shape[-1] // 2
    freqs = THETA ** (-jnp.arange(half, dtype=jnp.float32) * 2.0 / x.shape[-1])
    angles = positions.astype(jnp.float32)[:, None] * freqs[None, :]
    cosine = jnp.concatenate([jnp.cos(angles), jnp.cos(angles)], axis=-1)[:, None, :]
    sine = jnp.concatenate([jnp.sin(angles), jnp.sin(angles)], axis=-1)[:, None, :]
    turned = jnp.concatenate([-x[..., half:], x[..., :half]], axis=-1)
    return x * cosine + turned * sine

def request_info(index, lengths):
    ends = jnp.cumsum(lengths, dtype=jnp.int32)
    before = ends[None, :] <= index[:, None]
    segment = lax.optimization_barrier(jnp.sum(before.astype(jnp.int32), axis=1, dtype=jnp.int32))
    start = lax.optimization_barrier(jnp.sum(jnp.where(before, lengths[None, :], 0), axis=1, dtype=jnp.int32))
    return (segment, index - start)

def reference(tokens, attn_gain, qkv_weight, out_weight, prefix_cache, lengths, ffn_gain, expert_ids, gate_weights, expert_in, expert_out):
    groups = tokens.shape[0]
    suffix = tokens.shape[1]
    model = tokens.shape[2]
    head_cols = HEADS * HEAD_DIM
    kv_cols = KV_HEADS * HEAD_DIM
    ratio = HEADS // KV_HEADS
    prefix_len = prefix_cache.shape[1]
    scale = 1.0 / HEAD_DIM ** 0.5
    normed = rms_norm(tokens, attn_gain)
    qkv = jnp.dot(normed.reshape(-1, model), qkv_weight, preferred_element_type=jnp.float32).astype(jnp.bfloat16)
    qkv = qkv.reshape(groups, suffix, QKV_W)
    index = jnp.arange(suffix, dtype=jnp.int32)
    block = TOK_DEV
    reach_rows = REACH * block
    width = (REACH + 1) * block

    def per_group(operands):
        rows_qkv, lens, cache = operands
        segment, offset = request_info(index, lens)
        positions = prefix_len + offset
        query = rotary(rows_qkv[:, :head_cols].astype(jnp.float32).reshape(suffix, HEADS, HEAD_DIM), positions).astype(jnp.bfloat16)
        keys = rotary(rows_qkv[:, head_cols:head_cols + kv_cols].astype(jnp.float32).reshape(suffix, KV_HEADS, HEAD_DIM), positions).astype(jnp.bfloat16)
        values = rows_qkv[:, head_cols + kv_cols:].reshape(suffix, KV_HEADS, HEAD_DIM)
        keys_pad = jnp.pad(keys, ((reach_rows, 0), (0, 0), (0, 0)))
        values_pad = jnp.pad(values, ((reach_rows, 0), (0, 0), (0, 0)))
        pre_keys = cache[:, 0].astype(jnp.float32).reshape(prefix_len, KV_HEADS, HEAD_DIM)
        pre_values = cache[:, 1].astype(jnp.float32).reshape(prefix_len, KV_HEADS, HEAD_DIM)

        def one_block(number):
            start = (number * block).astype(jnp.int32)
            q_block = lax.dynamic_slice_in_dim(query, start, block, 0).astype(jnp.float32).reshape(block, KV_HEADS, ratio, HEAD_DIM)
            k_window = lax.dynamic_slice_in_dim(keys_pad, start, width, 0).astype(jnp.float32)
            v_window = lax.dynamic_slice_in_dim(values_pad, start, width, 0).astype(jnp.float32)
            q_index = start + jnp.arange(block, dtype=jnp.int32)
            k_index = start - reach_rows + jnp.arange(width, dtype=jnp.int32)
            q_segment = lax.dynamic_slice_in_dim(segment, start, block, 0)
            k_segment, unused = request_info(k_index, lens)
            visible = (k_index[None, :] >= 0) & (k_index[None, :] <= q_index[:, None]) & (k_segment[None, :] == q_segment[:, None])
            visible = visible[:, None, None, :]
            s_pre = jnp.einsum('tgrd,ngd->tgrn', q_block, pre_keys, precision=lax.Precision.HIGHEST) * scale
            s_suf = jnp.einsum('tgrd,ngd->tgrn', q_block, k_window, precision=lax.Precision.HIGHEST) * scale
            s_suf = jnp.where(visible, s_suf, -1e+30)
            best = jnp.maximum(lax.optimization_barrier(jnp.max(s_pre, axis=-1)), lax.optimization_barrier(jnp.max(s_suf, axis=-1)))
            p_pre = jnp.exp(s_pre - best[..., None])
            p_suf = jnp.where(visible, jnp.exp(s_suf - best[..., None]), 0.0)
            total = lax.optimization_barrier(jnp.sum(p_pre, axis=-1)) + lax.optimization_barrier(jnp.sum(p_suf, axis=-1))
            w_pre = lax.optimization_barrier(p_pre.astype(jnp.bfloat16)).astype(jnp.float32)
            w_suf = lax.optimization_barrier(p_suf.astype(jnp.bfloat16)).astype(jnp.float32)
            acc = jnp.einsum('tgrn,ngd->tgrd', w_pre, pre_values, precision=lax.Precision.HIGHEST)
            acc = acc + jnp.einsum('tgrn,ngd->tgrd', w_suf, v_window, precision=lax.Precision.HIGHEST)
            return (acc / total[..., None]).astype(jnp.bfloat16).reshape(block, head_cols)
        out = lax.map(one_block, jnp.arange(suffix // block, dtype=jnp.int32))
        return out.reshape(suffix, head_cols)
    attended = lax.map(per_group, (qkv, lengths, prefix_cache))
    projected = jnp.dot(attended.reshape(-1, head_cols), out_weight, preferred_element_type=jnp.float32)
    hidden_state = (tokens.reshape(-1, model).astype(jnp.float32) + projected).astype(jnp.bfloat16)
    moe_input = rms_norm(hidden_state, ffn_gain)
    all_tokens = moe_input.shape[0]
    unit_ff = expert_in.shape[2] // 2
    flat_ids = expert_ids.reshape(-1).astype(jnp.int32)
    flat_gates = gate_weights.reshape(-1)
    order = jnp.argsort(flat_ids, stable=True).astype(jnp.int32)
    counts = jnp.zeros((EXPERTS,), jnp.int32).at[flat_ids].add(1)
    starts = jnp.cumsum(counts, dtype=jnp.int32) - counts
    rows_block = 512
    order_pad = jnp.concatenate([order, jnp.zeros((rows_block,), jnp.int32)])

    def unit_step(unit, acc):
        expert = unit // SPLIT
        first = expert_in[unit]
        second = expert_out[unit]
        count = counts[expert]

        def block_step(number, acc):
            offset = (starts[expert] + number * rows_block).astype(jnp.int32)
            picks = lax.dynamic_slice_in_dim(order_pad, offset, rows_block, 0)
            live = number * rows_block + jnp.arange(rows_block, dtype=jnp.int32) < count
            token_rows = picks // TOPK
            inputs = moe_input[token_rows]
            inner = jnp.dot(inputs, first, preferred_element_type=jnp.float32)
            activated = (jax.nn.silu(inner[:, :unit_ff]) * inner[:, unit_ff:]).astype(jnp.bfloat16)
            produced = jnp.dot(activated, second, preferred_element_type=jnp.float32).astype(jnp.bfloat16)
            weight = jnp.where(live, flat_gates[picks], 0.0)
            return acc.at[token_rows].add(weight[:, None] * produced.astype(jnp.float32))
        return lax.fori_loop(0, (count + rows_block - 1) // rows_block, block_step, acc)
    combined = lax.fori_loop(0, UNITS, unit_step, jnp.zeros((all_tokens, model), jnp.float32))
    mixed = (hidden_state.astype(jnp.float32) + combined).astype(jnp.bfloat16)
    return (hidden_state.reshape(groups, suffix, model), mixed.reshape(groups, suffix, model))
```

```python
import jax
import jax.numpy as jnp
from jax import lax
from jax.sharding import PartitionSpec as P

HEADS = 24
KV_HEADS = 8
HEAD_DIM = 64
EXPERTS = 32
TOPK = 8
SHIFTS = 2
CAP = 40
TENSOR = ("chip", "core")


EPS = 1e-06
THETA = 10000.0


def from_behind(value, axis, steps):
    count = lax.axis_size(axis)
    first, last = (max(0, -steps), min(count, count - steps))
    return lax.ppermute(value, axis, [(source, source + steps) for source in range(first, last)])


def rms_norm(x, gain):
    values = x.astype(jnp.float32)
    mean_sq = jnp.mean(values * values, axis=-1, keepdims=True)
    return (values * lax.rsqrt(mean_sq + EPS) * gain).astype(jnp.bfloat16)


def rotary(x, positions):
    half = x.shape[-1] // 2
    freqs = THETA ** (-jnp.arange(half, dtype=jnp.float32) * 2.0 / x.shape[-1])
    angles = positions.astype(jnp.float32)[:, None] * freqs[None, :]
    cosine = jnp.concatenate([jnp.cos(angles), jnp.cos(angles)], axis=-1)[:, None, :]
    sine = jnp.concatenate([jnp.sin(angles), jnp.sin(angles)], axis=-1)[:, None, :]
    turned = jnp.concatenate([-x[..., half:], x[..., :half]], axis=-1)
    return x * cosine + turned * sine


def request_info(index, lengths):
    ends = jnp.cumsum(lengths, dtype=jnp.int32)
    before = ends[None, :] <= index[:, None]
    segment = jnp.sum(before.astype(jnp.int32), axis=1, dtype=jnp.int32)
    start = jnp.sum(jnp.where(before, lengths[None, :], 0), axis=1, dtype=jnp.int32)
    return (segment, index - start)


def merge_block(carry, scores, values, visible):
    best, total, acc = carry
    if visible is not None:
        scores = jnp.where(visible, scores, -1e30)
    newest = jnp.maximum(best, jnp.max(scores, axis=-1))
    probs = jnp.exp(scores - newest[..., None])
    if visible is not None:
        probs = jnp.where(visible, probs, 0.0)
    decay = jnp.exp(best - newest)
    total = total * decay + jnp.sum(probs, axis=-1)
    acc = acc * decay[..., None] + jnp.einsum(
        "tgrn,ngd->tgrd", probs.astype(jnp.bfloat16), values, preferred_element_type=jnp.float32
    )
    return (newest, total, acc)


def shards(
    tokens,
    attn_gain,
    qkv_weight,
    out_weight,
    prefix_cache,
    lengths,
    ffn_gain,
    expert_ids,
    gate_weights,
    expert_in,
    expert_out,
):
    rows = tokens.shape[1]
    model = tokens.shape[2]
    head_cols = HEADS * HEAD_DIM
    kv_cols = KV_HEADS * HEAD_DIM
    ratio = HEADS // KV_HEADS
    scale = 1.0 / HEAD_DIM**0.5
    lanes = lax.axis_size(TENSOR)
    prefix_len = prefix_cache.shape[1] * lanes
    own_lengths = lengths[0]
    inputs = tokens[0]
    normed = rms_norm(inputs, attn_gain)
    full_qkv, full_out = (
        lax.all_gather(qkv_weight, "dp", axis=1, tiled=True),
        lax.all_gather(out_weight, "dp", axis=0, tiled=True),
    )
    qkv = jnp.dot(normed, full_qkv, preferred_element_type=jnp.float32).astype(jnp.bfloat16)
    lane = lax.axis_index(TENSOR)
    q_index = lane * rows + jnp.arange(rows, dtype=jnp.int32)
    q_segment, offset = request_info(q_index, own_lengths)
    positions = prefix_len + offset
    query = rotary(
        qkv[:, :head_cols].astype(jnp.float32).reshape(rows, HEADS, HEAD_DIM), positions
    ).astype(jnp.bfloat16)
    query = query.reshape(rows, KV_HEADS, ratio, HEAD_DIM)
    keys = rotary(
        qkv[:, head_cols : head_cols + kv_cols]
        .astype(jnp.float32)
        .reshape(rows, KV_HEADS, HEAD_DIM),
        positions,
    ).astype(jnp.bfloat16)
    local_pairs = jnp.stack([keys.reshape(rows, kv_cols), qkv[:, head_cols + kv_cols :]], axis=1)
    start_carry = (
        jnp.full((rows, KV_HEADS, ratio), -1e30, jnp.float32),
        jnp.zeros((rows, KV_HEADS, ratio), jnp.float32),
        jnp.zeros((rows, KV_HEADS, ratio, HEAD_DIM), jnp.float32),
    )
    piece = lax.all_gather(prefix_cache[0], TENSOR, axis=0, tiled=True)
    count = piece.shape[0]
    cached_keys = piece[:, 0].reshape(count, KV_HEADS, HEAD_DIM)
    cached_values = piece[:, 1].reshape(count, KV_HEADS, HEAD_DIM)
    scores = (
        jnp.einsum("tgrd,ngd->tgrn", query, cached_keys, preferred_element_type=jnp.float32) * scale
    )
    carry = merge_block(start_carry, scores, cached_values, None)
    window = local_pairs[None]
    for bit in range(SHIFTS):
        earlier = from_behind(window, TENSOR, 2**bit)
        window = jnp.concatenate([window, earlier], axis=0)
    depth = window.shape[0]
    k_index = (
        (lane - jnp.arange(depth, dtype=jnp.int32))[:, None] * rows
        + jnp.arange(rows, dtype=jnp.int32)[None, :]
    ).reshape(-1)
    k_segment, unused = request_info(k_index, own_lengths)
    visible = (
        (k_index[None, :] >= 0)
        & (k_index[None, :] <= q_index[:, None])
        & (k_segment[None, :] == q_segment[:, None])
    )
    suffix_pairs = window.reshape(depth * rows, 2, kv_cols)
    suffix_keys = suffix_pairs[:, 0].reshape(depth * rows, KV_HEADS, HEAD_DIM)
    suffix_values = suffix_pairs[:, 1].reshape(depth * rows, KV_HEADS, HEAD_DIM)
    scores = (
        jnp.einsum("tgrd,ngd->tgrn", query, suffix_keys, preferred_element_type=jnp.float32) * scale
    )
    best, total, acc = merge_block(carry, scores, suffix_values, visible[:, None, None, :])
    attended = (acc / total[..., None]).astype(jnp.bfloat16).reshape(rows, head_cols)
    projected = jnp.dot(attended, full_out, preferred_element_type=jnp.float32)
    hidden_state = (inputs.astype(jnp.float32) + projected).astype(jnp.bfloat16)
    moe_input = rms_norm(hidden_state, ffn_gain)
    chips = lax.axis_size("chip")
    unit_ff = expert_in.shape[2] // 2
    flat_ids = expert_ids[0].reshape(-1)
    onehot = (flat_ids[:, None] == jnp.arange(EXPERTS, dtype=jnp.int32)[None, :]).astype(jnp.int32)
    earlier_count = jnp.cumsum(onehot, axis=0, dtype=jnp.int32) - onehot
    slots = jnp.sum(earlier_count * onehot, axis=1, dtype=jnp.int32)
    target = flat_ids * CAP + slots
    row_of = jnp.repeat(jnp.arange(rows, dtype=jnp.int32), TOPK)
    source = jnp.full((chips * CAP,), rows, jnp.int32).at[target].set(row_of)
    padded_input = jnp.concatenate([moe_input, jnp.zeros((1, model), jnp.bfloat16)], axis=0)
    outgoing = padded_input[source].reshape(chips, CAP, model)
    arrived = lax.all_to_all(outgoing, "chip", 0, 0, tiled=True)
    sibling = lax.ppermute(arrived, "core", [(0, 1), (1, 0)])
    unit_rows = jnp.concatenate([arrived, sibling], axis=0).reshape(2 * chips * CAP, model)
    inner = jnp.dot(unit_rows, expert_in[0], preferred_element_type=jnp.float32)
    activated = (jax.nn.silu(inner[:, :unit_ff]) * inner[:, unit_ff:]).astype(jnp.bfloat16)
    produced = jnp.dot(activated, expert_out[0], preferred_element_type=jnp.float32).astype(jnp.bfloat16)
    produced = produced.reshape(2, chips, CAP, model)
    partner = lax.ppermute(produced[1], "core", [(0, 1), (1, 0)])
    summed = (produced[0].astype(jnp.float32) + partner.astype(jnp.float32)).astype(jnp.bfloat16)
    returned = lax.all_to_all(summed, "chip", 0, 0, tiled=True)
    picked = returned.reshape(chips * CAP, model)[target].reshape(rows, TOPK, model)
    combined = jnp.einsum("tk,tkd->td", gate_weights[0], picked.astype(jnp.float32))
    mixed = (hidden_state.astype(jnp.float32) + combined).astype(jnp.bfloat16)
    return (hidden_state[None], mixed[None])


def solution(mesh):
    groups, lanes = mesh.devices.shape
    chip_mesh = jax.sharding.Mesh(mesh.devices.reshape(groups, lanes // 2, 2), ("dp", "chip", "core"))
    in_specs = (
        P("dp", TENSOR, None),
        P(),
        P(None, "dp"),
        P("dp", None),
        P("dp", TENSOR, None, None),
        P("dp", None),
        P(),
        P("dp", TENSOR, None),
        P("dp", TENSOR, None),
        P(TENSOR, None, None),
        P(TENSOR, None, None),
    )
    out_specs = (P("dp", TENSOR, None), P("dp", TENSOR, None))
    return jax.shard_map(shards, mesh=chip_mesh, in_specs=in_specs, out_specs=out_specs, check_vma=False)
```

```python
import jax
import jax.numpy as jnp
from jax import lax
from jax.sharding import PartitionSpec as P

HEADS = 24
KV_HEADS = 8
HEAD_DIM = 64
EXPERTS = 32
TOPK = 8
SHIFTS = 2
CAP = 40
TENSOR = ("chip", "core")


EPS = 1e-06
THETA = 10000.0


def from_behind(value, axis, steps):
    count = lax.axis_size(axis)
    first, last = (max(0, -steps), min(count, count - steps))
    return lax.ppermute(value, axis, [(source, source + steps) for source in range(first, last)])


def rms_norm(x, gain):
    values = x.astype(jnp.float32)
    mean_sq = jnp.mean(values * values, axis=-1, keepdims=True)
    return (values * lax.rsqrt(mean_sq + EPS) * gain).astype(jnp.bfloat16)


def rotary(x, positions):
    half = x.shape[-1] // 2
    freqs = THETA ** (-jnp.arange(half, dtype=jnp.float32) * 2.0 / x.shape[-1])
    angles = positions.astype(jnp.float32)[:, None] * freqs[None, :]
    cosine = jnp.concatenate([jnp.cos(angles), jnp.cos(angles)], axis=-1)[:, None, :]
    sine = jnp.concatenate([jnp.sin(angles), jnp.sin(angles)], axis=-1)[:, None, :]
    turned = jnp.concatenate([-x[..., half:], x[..., :half]], axis=-1)
    return x * cosine + turned * sine


def request_info(index, lengths):
    ends = jnp.cumsum(lengths, dtype=jnp.int32)
    before = ends[None, :] <= index[:, None]
    segment = jnp.sum(before.astype(jnp.int32), axis=1, dtype=jnp.int32)
    start = jnp.sum(jnp.where(before, lengths[None, :], 0), axis=1, dtype=jnp.int32)
    return (segment, index - start)


def merge_block(carry, scores, values, visible):
    best, total, acc = carry
    if visible is not None:
        scores = jnp.where(visible, scores, -1e30)
    newest = jnp.maximum(best, jnp.max(scores, axis=-1))
    probs = jnp.exp(scores - newest[..., None])
    if visible is not None:
        probs = jnp.where(visible, probs, 0.0)
    decay = jnp.exp(best - newest)
    total = total * decay + jnp.sum(probs, axis=-1)
    acc = acc * decay[..., None] + jnp.einsum(
        "tgrn,ngd->tgrd", probs.astype(jnp.bfloat16), values, preferred_element_type=jnp.float32
    )
    return (newest, total, acc)


def shards(
    tokens,
    attn_gain,
    qkv_weight,
    out_weight,
    prefix_cache,
    lengths,
    ffn_gain,
    expert_ids,
    gate_weights,
    expert_in,
    expert_out,
):
    rows = tokens.shape[1]
    model = tokens.shape[2]
    head_cols = HEADS * HEAD_DIM
    kv_cols = KV_HEADS * HEAD_DIM
    ratio = HEADS // KV_HEADS
    scale = 1.0 / HEAD_DIM**0.5
    lanes = lax.axis_size(TENSOR)
    prefix_len = prefix_cache.shape[1] * lanes
    own_lengths = lengths[0]
    inputs = tokens[0]
    normed = rms_norm(inputs, attn_gain)
    groups = lax.axis_size("dp")
    full_out = lax.all_gather(out_weight, "dp", axis=0, tiled=True)
    spread = jnp.broadcast_to(normed[None], (groups, rows, model))
    group_rows = lax.all_to_all(spread, "dp", 0, 0, tiled=True).reshape(groups * rows, model)
    qkv_part = jnp.dot(group_rows, qkv_weight, preferred_element_type=jnp.float32).astype(jnp.bfloat16)
    qkv_back = lax.all_to_all(qkv_part.reshape(groups, rows, -1), "dp", 0, 0, tiled=True)
    qkv = jnp.transpose(qkv_back, (1, 0, 2)).reshape(rows, -1)
    lane = lax.axis_index(TENSOR)
    q_index = lane * rows + jnp.arange(rows, dtype=jnp.int32)
    q_segment, offset = request_info(q_index, own_lengths)
    positions = prefix_len + offset
    query = rotary(
        qkv[:, :head_cols].astype(jnp.float32).reshape(rows, HEADS, HEAD_DIM), positions
    ).astype(jnp.bfloat16)
    query = query.reshape(rows, KV_HEADS, ratio, HEAD_DIM)
    keys = rotary(
        qkv[:, head_cols : head_cols + kv_cols]
        .astype(jnp.float32)
        .reshape(rows, KV_HEADS, HEAD_DIM),
        positions,
    ).astype(jnp.bfloat16)
    local_pairs = jnp.stack([keys.reshape(rows, kv_cols), qkv[:, head_cols + kv_cols :]], axis=1)
    start_carry = (
        jnp.full((rows, KV_HEADS, ratio), -1e30, jnp.float32),
        jnp.zeros((rows, KV_HEADS, ratio), jnp.float32),
        jnp.zeros((rows, KV_HEADS, ratio, HEAD_DIM), jnp.float32),
    )
    window = local_pairs[None]
    for bit in range(SHIFTS):
        earlier = from_behind(window, TENSOR, 2**bit)
        window = jnp.concatenate([window, earlier], axis=0)
    depth = window.shape[0]
    k_index = (
        (lane - jnp.arange(depth, dtype=jnp.int32))[:, None] * rows
        + jnp.arange(rows, dtype=jnp.int32)[None, :]
    ).reshape(-1)
    k_segment, unused = request_info(k_index, own_lengths)
    visible = (
        (k_index[None, :] >= 0)
        & (k_index[None, :] <= q_index[:, None])
        & (k_segment[None, :] == q_segment[:, None])
    )
    suffix_pairs = window.reshape(depth * rows, 2, kv_cols)
    suffix_keys = suffix_pairs[:, 0].reshape(depth * rows, KV_HEADS, HEAD_DIM)
    suffix_values = suffix_pairs[:, 1].reshape(depth * rows, KV_HEADS, HEAD_DIM)
    scores = (
        jnp.einsum("tgrd,ngd->tgrn", query, suffix_keys, preferred_element_type=jnp.float32) * scale
    )
    carry = merge_block(start_carry, scores, suffix_values, visible[:, None, None, :])
    piece = lax.all_gather(prefix_cache[0], TENSOR, axis=0, tiled=True)
    count = piece.shape[0]
    cached_keys = piece[:, 0].reshape(count, KV_HEADS, HEAD_DIM)
    cached_values = piece[:, 1].reshape(count, KV_HEADS, HEAD_DIM)
    scores = (
        jnp.einsum("tgrd,ngd->tgrn", query, cached_keys, preferred_element_type=jnp.float32) * scale
    )
    best, total, acc = merge_block(carry, scores, cached_values, None)
    attended = (acc / total[..., None]).astype(jnp.bfloat16).reshape(rows, head_cols)
    projected = jnp.dot(attended, full_out, preferred_element_type=jnp.float32)
    hidden_state = (inputs.astype(jnp.float32) + projected).astype(jnp.bfloat16)
    moe_input = rms_norm(hidden_state, ffn_gain)
    chips = lax.axis_size("chip")
    unit_ff = expert_in.shape[2] // 2
    flat_ids = expert_ids[0].reshape(-1)
    onehot = (flat_ids[:, None] == jnp.arange(EXPERTS, dtype=jnp.int32)[None, :]).astype(jnp.int32)
    earlier_count = jnp.cumsum(onehot, axis=0, dtype=jnp.int32) - onehot
    slots = jnp.sum(earlier_count * onehot, axis=1, dtype=jnp.int32)
    target = flat_ids * CAP + slots
    row_of = jnp.repeat(jnp.arange(rows, dtype=jnp.int32), TOPK)
    source = jnp.full((chips * CAP,), rows, jnp.int32).at[target].set(row_of)
    padded_input = jnp.concatenate([moe_input, jnp.zeros((1, model), jnp.bfloat16)], axis=0)
    outgoing = padded_input[source].reshape(chips, CAP, model)
    arrived = lax.all_to_all(outgoing, "chip", 0, 0, tiled=True)
    sibling = lax.ppermute(arrived, "core", [(0, 1), (1, 0)])
    unit_rows = jnp.concatenate([arrived, sibling], axis=0).reshape(2 * chips * CAP, model)
    inner = jnp.dot(unit_rows, expert_in[0], preferred_element_type=jnp.float32)
    activated = (jax.nn.silu(inner[:, :unit_ff]) * inner[:, unit_ff:]).astype(jnp.bfloat16)
    produced = jnp.dot(activated, expert_out[0], preferred_element_type=jnp.float32).astype(jnp.bfloat16)
    produced = produced.reshape(2, chips, CAP, model)
    partner = lax.ppermute(produced[1], "core", [(0, 1), (1, 0)])
    summed = (produced[0].astype(jnp.float32) + partner.astype(jnp.float32)).astype(jnp.bfloat16)
    returned = lax.all_to_all(summed, "chip", 0, 0, tiled=True)
    picked = returned.reshape(chips * CAP, model)[target].reshape(rows, TOPK, model)
    combined = jnp.einsum("tk,tkd->td", gate_weights[0], picked.astype(jnp.float32))
    mixed = (hidden_state.astype(jnp.float32) + combined).astype(jnp.bfloat16)
    return (hidden_state[None], mixed[None])


def solution(mesh):
    groups, lanes = mesh.devices.shape
    chip_mesh = jax.sharding.Mesh(mesh.devices.reshape(groups, lanes // 2, 2), ("dp", "chip", "core"))
    in_specs = (
        P("dp", TENSOR, None),
        P(),
        P(None, "dp"),
        P("dp", None),
        P("dp", TENSOR, None, None),
        P("dp", None),
        P(),
        P("dp", TENSOR, None),
        P("dp", TENSOR, None),
        P(TENSOR, None, None),
        P(TENSOR, None, None),
    )
    out_specs = (P("dp", TENSOR, None), P("dp", TENSOR, None))
    return jax.shard_map(shards, mesh=chip_mesh, in_specs=in_specs, out_specs=out_specs, check_vma=False)
```

```python
import jax
import jax.numpy as jnp
from jax import lax
from jax.sharding import PartitionSpec as P

HEADS = 24
KV_HEADS = 8
HEAD_DIM = 64
EXPERTS = 32
TOPK = 8
SHIFTS = 2
CAP = 40
TENSOR = ("chip", "core")


EPS = 1e-06
THETA = 10000.0


def from_behind(value, axis, steps):
    count = lax.axis_size(axis)
    first, last = (max(0, -steps), min(count, count - steps))
    return lax.ppermute(value, axis, [(source, source + steps) for source in range(first, last)])


def rms_norm(x, gain):
    values = x.astype(jnp.float32)
    mean_sq = jnp.mean(values * values, axis=-1, keepdims=True)
    return (values * lax.rsqrt(mean_sq + EPS) * gain).astype(jnp.bfloat16)


def rotary(x, positions):
    half = x.shape[-1] // 2
    freqs = THETA ** (-jnp.arange(half, dtype=jnp.float32) * 2.0 / x.shape[-1])
    angles = positions.astype(jnp.float32)[:, None] * freqs[None, :]
    cosine = jnp.concatenate([jnp.cos(angles), jnp.cos(angles)], axis=-1)[:, None, :]
    sine = jnp.concatenate([jnp.sin(angles), jnp.sin(angles)], axis=-1)[:, None, :]
    turned = jnp.concatenate([-x[..., half:], x[..., :half]], axis=-1)
    return x * cosine + turned * sine


def request_info(index, lengths):
    ends = jnp.cumsum(lengths, dtype=jnp.int32)
    before = ends[None, :] <= index[:, None]
    segment = jnp.sum(before.astype(jnp.int32), axis=1, dtype=jnp.int32)
    start = jnp.sum(jnp.where(before, lengths[None, :], 0), axis=1, dtype=jnp.int32)
    return (segment, index - start)


def merge_block(carry, scores, values, visible):
    best, total, acc = carry
    if visible is not None:
        scores = jnp.where(visible, scores, -1e30)
    newest = jnp.maximum(best, jnp.max(scores, axis=-1))
    probs = jnp.exp(scores - newest[..., None])
    if visible is not None:
        probs = jnp.where(visible, probs, 0.0)
    decay = jnp.exp(best - newest)
    total = total * decay + jnp.sum(probs, axis=-1)
    acc = acc * decay[..., None] + jnp.einsum(
        "tgrn,ngd->tgrd", probs.astype(jnp.bfloat16), values, preferred_element_type=jnp.float32
    )
    return (newest, total, acc)


def shards(
    tokens,
    attn_gain,
    qkv_weight,
    out_weight,
    prefix_cache,
    lengths,
    ffn_gain,
    expert_ids,
    gate_weights,
    expert_in,
    expert_out,
):
    rows = tokens.shape[1]
    model = tokens.shape[2]
    head_cols = HEADS * HEAD_DIM
    kv_cols = KV_HEADS * HEAD_DIM
    ratio = HEADS // KV_HEADS
    scale = 1.0 / HEAD_DIM**0.5
    lanes = lax.axis_size(TENSOR)
    prefix_len = prefix_cache.shape[1] * lanes
    own_lengths = lengths[0]
    inputs = tokens[0]
    normed = rms_norm(inputs, attn_gain)
    groups = lax.axis_size("dp")
    out_spread = jnp.broadcast_to(out_weight[None], (groups,) + out_weight.shape)
    full_out = lax.all_to_all(out_spread, "dp", 0, 0, tiled=True).reshape(groups * out_weight.shape[0], -1)
    spread = jnp.broadcast_to(normed[None], (groups, rows, model))
    group_rows = lax.all_to_all(spread, "dp", 0, 0, tiled=True).reshape(groups * rows, model)
    qkv_part = jnp.dot(group_rows, qkv_weight, preferred_element_type=jnp.float32).astype(jnp.bfloat16)
    qkv_back = lax.all_to_all(qkv_part.reshape(groups, rows, -1), "dp", 0, 0, tiled=True)
    qkv = jnp.transpose(qkv_back, (1, 0, 2)).reshape(rows, -1)
    lane = lax.axis_index(TENSOR)
    q_index = lane * rows + jnp.arange(rows, dtype=jnp.int32)
    q_segment, offset = request_info(q_index, own_lengths)
    positions = prefix_len + offset
    query = rotary(
        qkv[:, :head_cols].astype(jnp.float32).reshape(rows, HEADS, HEAD_DIM), positions
    ).astype(jnp.bfloat16)
    query = query.reshape(rows, KV_HEADS, ratio, HEAD_DIM)
    keys = rotary(
        qkv[:, head_cols : head_cols + kv_cols]
        .astype(jnp.float32)
        .reshape(rows, KV_HEADS, HEAD_DIM),
        positions,
    ).astype(jnp.bfloat16)
    local_pairs = jnp.stack([keys.reshape(rows, kv_cols), qkv[:, head_cols + kv_cols :]], axis=1)
    start_carry = (
        jnp.full((rows, KV_HEADS, ratio), -1e30, jnp.float32),
        jnp.zeros((rows, KV_HEADS, ratio), jnp.float32),
        jnp.zeros((rows, KV_HEADS, ratio, HEAD_DIM), jnp.float32),
    )
    window = local_pairs[None]
    for bit in range(SHIFTS):
        earlier = from_behind(window, TENSOR, 2**bit)
        window = jnp.concatenate([window, earlier], axis=0)
    depth = window.shape[0]
    k_index = (
        (lane - jnp.arange(depth, dtype=jnp.int32))[:, None] * rows
        + jnp.arange(rows, dtype=jnp.int32)[None, :]
    ).reshape(-1)
    k_segment, unused = request_info(k_index, own_lengths)
    visible = (
        (k_index[None, :] >= 0)
        & (k_index[None, :] <= q_index[:, None])
        & (k_segment[None, :] == q_segment[:, None])
    )
    suffix_pairs = window.reshape(depth * rows, 2, kv_cols)
    suffix_keys = suffix_pairs[:, 0].reshape(depth * rows, KV_HEADS, HEAD_DIM)
    suffix_values = suffix_pairs[:, 1].reshape(depth * rows, KV_HEADS, HEAD_DIM)
    scores = (
        jnp.einsum("tgrd,ngd->tgrn", query, suffix_keys, preferred_element_type=jnp.float32) * scale
    )
    carry = merge_block(start_carry, scores, suffix_values, visible[:, None, None, :])
    piece = lax.all_gather(prefix_cache[0], TENSOR, axis=0, tiled=True)
    count = piece.shape[0]
    cached_keys = piece[:, 0].reshape(count, KV_HEADS, HEAD_DIM)
    cached_values = piece[:, 1].reshape(count, KV_HEADS, HEAD_DIM)
    scores = (
        jnp.einsum("tgrd,ngd->tgrn", query, cached_keys, preferred_element_type=jnp.float32) * scale
    )
    best, total, acc = merge_block(carry, scores, cached_values, None)
    attended = (acc / total[..., None]).astype(jnp.bfloat16).reshape(rows, head_cols)
    projected = jnp.dot(attended, full_out, preferred_element_type=jnp.float32)
    hidden_state = (inputs.astype(jnp.float32) + projected).astype(jnp.bfloat16)
    moe_input = rms_norm(hidden_state, ffn_gain)
    chips = lax.axis_size("chip")
    unit_ff = expert_in.shape[2] // 2
    own_ids = expert_ids[0]
    flat_ids = own_ids.reshape(-1)
    named = jnp.sum(
        (own_ids[:, :, None] == jnp.arange(EXPERTS, dtype=jnp.int32)[None, None, :]).astype(jnp.float32), axis=1
    )
    order = jnp.arange(rows, dtype=jnp.int32)
    below = (order[None, :] < order[:, None]).astype(jnp.bfloat16)
    earlier = jnp.dot(below, named.astype(jnp.bfloat16), preferred_element_type=jnp.float32)
    slots = jnp.take_along_axis(earlier, own_ids, axis=1).astype(jnp.int32).reshape(-1)
    target = flat_ids * CAP + slots
    row_of = jnp.repeat(jnp.arange(rows, dtype=jnp.int32), TOPK)
    source = jnp.full((chips * CAP,), rows, jnp.int32).at[target].set(row_of)
    padded_input = jnp.concatenate([moe_input, jnp.zeros((1, model), jnp.bfloat16)], axis=0)
    outgoing = padded_input[source].reshape(chips, CAP, model)
    arrived = lax.all_to_all(outgoing, "chip", 0, 0, tiled=True)
    sibling = lax.ppermute(arrived, "core", [(0, 1), (1, 0)])

    def unit(block):
        inner = jnp.dot(block.reshape(chips * CAP, model), expert_in[0], preferred_element_type=jnp.float32)
        activated = (jax.nn.silu(inner[:, :unit_ff]) * inner[:, unit_ff:]).astype(jnp.bfloat16)
        produced = jnp.dot(activated, expert_out[0], preferred_element_type=jnp.float32).astype(jnp.bfloat16)
        return produced.reshape(chips, CAP, model)

    own_part = unit(arrived)
    partner = lax.ppermute(unit(sibling), "core", [(0, 1), (1, 0)])
    summed = (own_part.astype(jnp.float32) + partner.astype(jnp.float32)).astype(jnp.bfloat16)
    returned = lax.all_to_all(summed, "chip", 0, 0, tiled=True)
    picked = returned.reshape(chips * CAP, model)[target].reshape(rows, TOPK, model)
    combined = jnp.einsum("tk,tkd->td", gate_weights[0], picked.astype(jnp.float32))
    mixed = (hidden_state.astype(jnp.float32) + combined).astype(jnp.bfloat16)
    return (hidden_state[None], mixed[None])


def solution(mesh):
    groups, lanes = mesh.devices.shape
    chip_mesh = jax.sharding.Mesh(mesh.devices.reshape(groups, lanes // 2, 2), ("dp", "chip", "core"))
    in_specs = (
        P("dp", TENSOR, None),
        P(),
        P(None, "dp"),
        P("dp", None),
        P("dp", TENSOR, None, None),
        P("dp", None),
        P(),
        P("dp", TENSOR, None),
        P("dp", TENSOR, None),
        P(TENSOR, None, None),
        P(TENSOR, None, None),
    )
    out_specs = (P("dp", TENSOR, None), P("dp", TENSOR, None))
    return jax.shard_map(shards, mesh=chip_mesh, in_specs=in_specs, out_specs=out_specs, check_vma=False)
```

```python
import jax
import jax.numpy as jnp
from jax import lax
from jax.sharding import PartitionSpec as P

HEADS = 24
KV_HEADS = 8
HEAD_DIM = 64
EXPERTS = 32
TOPK = 8
SHIFTS = 2
CAP = 40
TENSOR = ("chip", "core")


EPS = 1e-06
THETA = 10000.0


def from_behind(value, axis, steps):
    count = lax.axis_size(axis)
    first, last = (max(0, -steps), min(count, count - steps))
    return lax.ppermute(value, axis, [(source, source + steps) for source in range(first, last)])


def rms_norm(x, gain):
    values = x.astype(jnp.float32)
    mean_sq = jnp.mean(values * values, axis=-1, keepdims=True)
    return (values * lax.rsqrt(mean_sq + EPS) * gain).astype(jnp.bfloat16)


def rotary(x, positions):
    half = x.shape[-1] // 2
    freqs = THETA ** (-jnp.arange(half, dtype=jnp.float32) * 2.0 / x.shape[-1])
    angles = positions.astype(jnp.float32)[:, None] * freqs[None, :]
    cosine = jnp.concatenate([jnp.cos(angles), jnp.cos(angles)], axis=-1)[:, None, :]
    sine = jnp.concatenate([jnp.sin(angles), jnp.sin(angles)], axis=-1)[:, None, :]
    turned = jnp.concatenate([-x[..., half:], x[..., :half]], axis=-1)
    return x * cosine + turned * sine


def request_info(index, lengths):
    ends = jnp.cumsum(lengths, dtype=jnp.int32)
    before = ends[None, :] <= index[:, None]
    segment = jnp.sum(before.astype(jnp.int32), axis=1, dtype=jnp.int32)
    start = jnp.sum(jnp.where(before, lengths[None, :], 0), axis=1, dtype=jnp.int32)
    return (segment, index - start)


def merge_block(carry, scores, values, visible):
    best, total, acc = carry
    if visible is not None:
        scores = jnp.where(visible, scores, -1e30)
    newest = jnp.maximum(best, jnp.max(scores, axis=-1))
    probs = jnp.exp(scores - newest[..., None])
    if visible is not None:
        probs = jnp.where(visible, probs, 0.0)
    decay = jnp.exp(best - newest)
    total = total * decay + jnp.sum(probs, axis=-1)
    acc = acc * decay[..., None] + jnp.einsum(
        "tgrn,ngd->tgrd", probs.astype(jnp.bfloat16), values, preferred_element_type=jnp.float32
    )
    return (newest, total, acc)


def shards(
    tokens,
    attn_gain,
    qkv_weight,
    out_weight,
    prefix_cache,
    lengths,
    ffn_gain,
    expert_ids,
    gate_weights,
    expert_in,
    expert_out,
):
    rows = tokens.shape[1]
    model = tokens.shape[2]
    head_cols = HEADS * HEAD_DIM
    kv_cols = KV_HEADS * HEAD_DIM
    ratio = HEADS // KV_HEADS
    scale = 1.0 / HEAD_DIM**0.5
    lanes = lax.axis_size(TENSOR)
    prefix_len = prefix_cache.shape[1] * lanes
    own_lengths = lengths[0]
    inputs = tokens[0]
    normed = rms_norm(inputs, attn_gain)
    groups = lax.axis_size("dp")
    out_spread = jnp.broadcast_to(out_weight[None], (groups,) + out_weight.shape)
    full_out = lax.all_to_all(out_spread, "dp", 0, 0, tiled=True).reshape(groups * out_weight.shape[0], -1)
    spread = jnp.broadcast_to(normed[None], (groups, rows, model))
    group_rows = lax.all_to_all(spread, "dp", 0, 0, tiled=True).reshape(groups * rows, model)
    qkv_part = jnp.dot(group_rows, qkv_weight, preferred_element_type=jnp.float32).astype(jnp.bfloat16)
    qkv_back = lax.all_to_all(qkv_part.reshape(groups, rows, -1), "dp", 0, 0, tiled=True)
    qkv = jnp.transpose(qkv_back, (1, 0, 2)).reshape(rows, -1)
    lane = lax.axis_index(TENSOR)
    q_index = lane * rows + jnp.arange(rows, dtype=jnp.int32)
    q_segment, offset = request_info(q_index, own_lengths)
    positions = prefix_len + offset
    query = rotary(
        qkv[:, :head_cols].astype(jnp.float32).reshape(rows, HEADS, HEAD_DIM), positions
    ).astype(jnp.bfloat16)
    query = query.reshape(rows, KV_HEADS, ratio, HEAD_DIM)
    keys = rotary(
        qkv[:, head_cols : head_cols + kv_cols]
        .astype(jnp.float32)
        .reshape(rows, KV_HEADS, HEAD_DIM),
        positions,
    ).astype(jnp.bfloat16)
    local_pairs = jnp.stack([keys.reshape(rows, kv_cols), qkv[:, head_cols + kv_cols :]], axis=1)
    start_carry = (
        jnp.full((rows, KV_HEADS, ratio), -1e30, jnp.float32),
        jnp.zeros((rows, KV_HEADS, ratio), jnp.float32),
        jnp.zeros((rows, KV_HEADS, ratio, HEAD_DIM), jnp.float32),
    )
    window = jnp.stack([local_pairs] + [from_behind(local_pairs, TENSOR, step) for step in range(1, 2**SHIFTS)])
    depth = window.shape[0]
    k_index = (
        (lane - jnp.arange(depth, dtype=jnp.int32))[:, None] * rows
        + jnp.arange(rows, dtype=jnp.int32)[None, :]
    ).reshape(-1)
    k_segment, unused = request_info(k_index, own_lengths)
    visible = (
        (k_index[None, :] >= 0)
        & (k_index[None, :] <= q_index[:, None])
        & (k_segment[None, :] == q_segment[:, None])
    )
    suffix_pairs = window.reshape(depth * rows, 2, kv_cols)
    suffix_keys = suffix_pairs[:, 0].reshape(depth * rows, KV_HEADS, HEAD_DIM)
    suffix_values = suffix_pairs[:, 1].reshape(depth * rows, KV_HEADS, HEAD_DIM)
    scores = (
        jnp.einsum("tgrd,ngd->tgrn", query, suffix_keys, preferred_element_type=jnp.float32) * scale
    )
    carry = merge_block(start_carry, scores, suffix_values, visible[:, None, None, :])
    cache_spread = jnp.broadcast_to(prefix_cache[0][None], (lanes,) + prefix_cache.shape[1:])
    piece = lax.all_to_all(cache_spread, TENSOR, 0, 0, tiled=True).reshape((prefix_len,) + prefix_cache.shape[2:])
    count = piece.shape[0]
    cached_keys = piece[:, 0].reshape(count, KV_HEADS, HEAD_DIM)
    cached_values = piece[:, 1].reshape(count, KV_HEADS, HEAD_DIM)
    scores = (
        jnp.einsum("tgrd,ngd->tgrn", query, cached_keys, preferred_element_type=jnp.float32) * scale
    )
    best, total, acc = merge_block(carry, scores, cached_values, None)
    attended = (acc / total[..., None]).astype(jnp.bfloat16).reshape(rows, head_cols)
    projected = jnp.dot(attended, full_out, preferred_element_type=jnp.float32)
    hidden_state = (inputs.astype(jnp.float32) + projected).astype(jnp.bfloat16)
    moe_input = rms_norm(hidden_state, ffn_gain)
    chips = lax.axis_size("chip")
    unit_ff = expert_in.shape[2] // 2
    own_ids = expert_ids[0]
    flat_ids = own_ids.reshape(-1)
    named = jnp.sum(
        (own_ids[:, :, None] == jnp.arange(EXPERTS, dtype=jnp.int32)[None, None, :]).astype(jnp.float32), axis=1
    )
    order = jnp.arange(rows, dtype=jnp.int32)
    below = (order[None, :] < order[:, None]).astype(jnp.bfloat16)
    earlier = jnp.dot(below, named.astype(jnp.bfloat16), preferred_element_type=jnp.float32)
    slots = jnp.take_along_axis(earlier, own_ids, axis=1).astype(jnp.int32).reshape(-1)
    target = flat_ids * CAP + slots
    row_of = jnp.repeat(jnp.arange(rows, dtype=jnp.int32), TOPK)
    source = jnp.full((chips * CAP,), rows, jnp.int32).at[target].set(row_of)
    padded_input = jnp.concatenate([moe_input, jnp.zeros((1, model), jnp.bfloat16)], axis=0)
    outgoing = padded_input[source].reshape(chips, CAP, model)
    arrived = lax.all_to_all(outgoing, "chip", 0, 0, tiled=True)
    sibling = lax.ppermute(arrived, "core", [(0, 1), (1, 0)])

    def unit(block):
        inner = jnp.dot(block.reshape(chips * CAP, model), expert_in[0], preferred_element_type=jnp.float32)
        activated = (jax.nn.silu(inner[:, :unit_ff]) * inner[:, unit_ff:]).astype(jnp.bfloat16)
        produced = jnp.dot(activated, expert_out[0], preferred_element_type=jnp.float32).astype(jnp.bfloat16)
        return produced.reshape(chips, CAP, model)

    own_part = unit(arrived)
    partner = lax.ppermute(unit(sibling), "core", [(0, 1), (1, 0)])
    summed = (own_part.astype(jnp.float32) + partner.astype(jnp.float32)).astype(jnp.bfloat16)
    returned = lax.all_to_all(summed, "chip", 0, 0, tiled=True)
    picked = returned.reshape(chips * CAP, model)[target].reshape(rows, TOPK, model)
    combined = jnp.einsum("tk,tkd->td", gate_weights[0], picked.astype(jnp.float32))
    mixed = (hidden_state.astype(jnp.float32) + combined).astype(jnp.bfloat16)
    return (hidden_state[None], mixed[None])


def solution(mesh):
    groups, lanes = mesh.devices.shape
    chip_mesh = jax.sharding.Mesh(mesh.devices.reshape(groups, lanes // 2, 2), ("dp", "chip", "core"))
    in_specs = (
        P("dp", TENSOR, None),
        P(),
        P(None, "dp"),
        P("dp", None),
        P("dp", TENSOR, None, None),
        P("dp", None),
        P(),
        P("dp", TENSOR, None),
        P("dp", TENSOR, None),
        P(TENSOR, None, None),
        P(TENSOR, None, None),
    )
    out_specs = (P("dp", TENSOR, None), P("dp", TENSOR, None))
    return jax.shard_map(shards, mesh=chip_mesh, in_specs=in_specs, out_specs=out_specs, check_vma=False)
```

```python
import jax
import jax.numpy as jnp
from jax import lax
from jax.sharding import PartitionSpec as P

HEADS = 24
KV_HEADS = 8
HEAD_DIM = 64
EXPERTS = 32
TOPK = 8
SHIFTS = 2
CAP = 40
TENSOR = ("chip", "core")


EPS = 1e-06
THETA = 10000.0


def from_behind(value, axis, steps):
    count = lax.axis_size(axis)
    first, last = (max(0, -steps), min(count, count - steps))
    return lax.ppermute(value, axis, [(source, source + steps) for source in range(first, last)])


def rms_norm(x, gain):
    values = x.astype(jnp.float32)
    mean_sq = jnp.mean(values * values, axis=-1, keepdims=True)
    return (values * lax.rsqrt(mean_sq + EPS) * gain).astype(jnp.bfloat16)


def rotary(x, positions):
    half = x.shape[-1] // 2
    freqs = THETA ** (-jnp.arange(half, dtype=jnp.float32) * 2.0 / x.shape[-1])
    angles = positions.astype(jnp.float32)[:, None] * freqs[None, :]
    cosine = jnp.concatenate([jnp.cos(angles), jnp.cos(angles)], axis=-1)[:, None, :]
    sine = jnp.concatenate([jnp.sin(angles), jnp.sin(angles)], axis=-1)[:, None, :]
    turned = jnp.concatenate([-x[..., half:], x[..., :half]], axis=-1)
    return x * cosine + turned * sine


def request_info(index, lengths):
    ends = jnp.cumsum(lengths, dtype=jnp.int32)
    before = ends[None, :] <= index[:, None]
    segment = jnp.sum(before.astype(jnp.int32), axis=1, dtype=jnp.int32)
    start = jnp.sum(jnp.where(before, lengths[None, :], 0), axis=1, dtype=jnp.int32)
    return (segment, index - start)


def merge_block(carry, scores, values, visible):
    best, total, acc = carry
    if visible is not None:
        scores = jnp.where(visible, scores, -1e30)
    newest = jnp.maximum(best, jnp.max(scores, axis=-1))
    probs = jnp.exp(scores - newest[..., None])
    if visible is not None:
        probs = jnp.where(visible, probs, 0.0)
    decay = jnp.exp(best - newest)
    total = total * decay + jnp.sum(probs, axis=-1)
    acc = acc * decay[..., None] + jnp.einsum(
        "tgrn,ngd->tgrd", probs.astype(jnp.bfloat16), values, preferred_element_type=jnp.float32
    )
    return (newest, total, acc)


def shards(
    tokens,
    attn_gain,
    qkv_weight,
    out_weight,
    prefix_cache,
    lengths,
    ffn_gain,
    expert_ids,
    gate_weights,
    expert_in,
    expert_out,
):
    rows = tokens.shape[1]
    model = tokens.shape[2]
    head_cols = HEADS * HEAD_DIM
    kv_cols = KV_HEADS * HEAD_DIM
    ratio = HEADS // KV_HEADS
    scale = 1.0 / HEAD_DIM**0.5
    lanes = lax.axis_size(TENSOR)
    prefix_len = prefix_cache.shape[1] * lanes
    own_lengths = lengths[0]
    inputs = tokens[0]
    normed = rms_norm(inputs, attn_gain)
    groups = lax.axis_size("dp")
    out_spread = jnp.broadcast_to(out_weight[None], (groups,) + out_weight.shape)
    full_out = lax.all_to_all(out_spread, "dp", 0, 0, tiled=True).reshape(groups * out_weight.shape[0], -1)
    spread = jnp.broadcast_to(normed[None], (groups, rows, model))
    group_rows = lax.all_to_all(spread, "dp", 0, 0, tiled=True).reshape(groups * rows, model)
    qkv_part = jnp.dot(group_rows, qkv_weight, preferred_element_type=jnp.float32).astype(jnp.bfloat16)
    qkv_back = lax.all_to_all(qkv_part.reshape(groups, rows, -1), "dp", 0, 0, tiled=True)
    qkv = jnp.transpose(qkv_back, (1, 0, 2)).reshape(rows, -1)
    lane = lax.axis_index(TENSOR)
    q_index = lane * rows + jnp.arange(rows, dtype=jnp.int32)
    q_segment, offset = request_info(q_index, own_lengths)
    positions = prefix_len + offset
    query = rotary(
        qkv[:, :head_cols].astype(jnp.float32).reshape(rows, HEADS, HEAD_DIM), positions
    ).astype(jnp.bfloat16)
    query = query.reshape(rows, KV_HEADS, ratio, HEAD_DIM)
    keys = rotary(
        qkv[:, head_cols : head_cols + kv_cols]
        .astype(jnp.float32)
        .reshape(rows, KV_HEADS, HEAD_DIM),
        positions,
    ).astype(jnp.bfloat16)
    local_pairs = jnp.stack([keys.reshape(rows, kv_cols), qkv[:, head_cols + kv_cols :]], axis=1)
    start_carry = (
        jnp.full((rows, KV_HEADS, ratio), -1e30, jnp.float32),
        jnp.zeros((rows, KV_HEADS, ratio), jnp.float32),
        jnp.zeros((rows, KV_HEADS, ratio, HEAD_DIM), jnp.float32),
    )
    window = local_pairs[None]
    for bit in range(SHIFTS):
        earlier = from_behind(window, TENSOR, 2**bit)
        window = jnp.concatenate([window, earlier], axis=0)
    depth = window.shape[0]
    k_index = (
        (lane - jnp.arange(depth, dtype=jnp.int32))[:, None] * rows
        + jnp.arange(rows, dtype=jnp.int32)[None, :]
    ).reshape(-1)
    k_segment, unused = request_info(k_index, own_lengths)
    visible = (
        (k_index[None, :] >= 0)
        & (k_index[None, :] <= q_index[:, None])
        & (k_segment[None, :] == q_segment[:, None])
    )
    suffix_pairs = window.reshape(depth * rows, 2, kv_cols)
    suffix_keys = suffix_pairs[:, 0].reshape(depth * rows, KV_HEADS, HEAD_DIM)
    suffix_values = suffix_pairs[:, 1].reshape(depth * rows, KV_HEADS, HEAD_DIM)
    scores = (
        jnp.einsum("tgrd,ngd->tgrn", query, suffix_keys, preferred_element_type=jnp.float32) * scale
    )
    carry = merge_block(start_carry, scores, suffix_values, visible[:, None, None, :])
    piece = lax.all_gather(prefix_cache[0], TENSOR, axis=0, tiled=True)
    piece, carry = lax.optimization_barrier((piece, carry))
    count = piece.shape[0]
    cached_keys = piece[:, 0].reshape(count, KV_HEADS, HEAD_DIM)
    cached_values = piece[:, 1].reshape(count, KV_HEADS, HEAD_DIM)
    scores = (
        jnp.einsum("tgrd,ngd->tgrn", query, cached_keys, preferred_element_type=jnp.float32) * scale
    )
    best, total, acc = merge_block(carry, scores, cached_values, None)
    attended = (acc / total[..., None]).astype(jnp.bfloat16).reshape(rows, head_cols)
    projected = jnp.dot(attended, full_out, preferred_element_type=jnp.float32)
    hidden_state = (inputs.astype(jnp.float32) + projected).astype(jnp.bfloat16)
    moe_input = rms_norm(hidden_state, ffn_gain)
    chips = lax.axis_size("chip")
    unit_ff = expert_in.shape[2] // 2
    own_ids = expert_ids[0]
    flat_ids = own_ids.reshape(-1)
    named = jnp.sum(
        (own_ids[:, :, None] == jnp.arange(EXPERTS, dtype=jnp.int32)[None, None, :]).astype(jnp.float32), axis=1
    )
    order = jnp.arange(rows, dtype=jnp.int32)
    below = (order[None, :] < order[:, None]).astype(jnp.bfloat16)
    earlier = jnp.dot(below, named.astype(jnp.bfloat16), preferred_element_type=jnp.float32)
    slots = jnp.take_along_axis(earlier, own_ids, axis=1).astype(jnp.int32).reshape(-1)
    target = flat_ids * CAP + slots
    row_of = jnp.repeat(jnp.arange(rows, dtype=jnp.int32), TOPK)
    source = jnp.full((chips * CAP,), rows, jnp.int32).at[target].set(row_of)
    padded_input = jnp.concatenate([moe_input, jnp.zeros((1, model), jnp.bfloat16)], axis=0)
    outgoing = padded_input[source].reshape(chips, CAP, model)
    arrived = lax.all_to_all(outgoing, "chip", 0, 0, tiled=True)
    sibling = lax.ppermute(arrived, "core", [(0, 1), (1, 0)])

    def unit(block):
        inner = jnp.dot(block.reshape(chips * CAP, model), expert_in[0], preferred_element_type=jnp.float32)
        activated = (jax.nn.silu(inner[:, :unit_ff]) * inner[:, unit_ff:]).astype(jnp.bfloat16)
        produced = jnp.dot(activated, expert_out[0], preferred_element_type=jnp.float32).astype(jnp.bfloat16)
        return produced.reshape(chips, CAP, model)

    own_part = unit(arrived)
    partner = lax.ppermute(unit(sibling), "core", [(0, 1), (1, 0)])
    summed = (own_part.astype(jnp.float32) + partner.astype(jnp.float32)).astype(jnp.bfloat16)
    returned = lax.all_to_all(summed, "chip", 0, 0, tiled=True)
    picked = returned.reshape(chips * CAP, model)[target].reshape(rows, TOPK, model)
    combined = jnp.einsum("tk,tkd->td", gate_weights[0], picked.astype(jnp.float32))
    mixed = (hidden_state.astype(jnp.float32) + combined).astype(jnp.bfloat16)
    return (hidden_state[None], mixed[None])


def solution(mesh):
    groups, lanes = mesh.devices.shape
    chip_mesh = jax.sharding.Mesh(mesh.devices.reshape(groups, lanes // 2, 2), ("dp", "chip", "core"))
    in_specs = (
        P("dp", TENSOR, None),
        P(),
        P(None, "dp"),
        P("dp", None),
        P("dp", TENSOR, None, None),
        P("dp", None),
        P(),
        P("dp", TENSOR, None),
        P("dp", TENSOR, None),
        P(TENSOR, None, None),
        P(TENSOR, None, None),
    )
    out_specs = (P("dp", TENSOR, None), P("dp", TENSOR, None))
    return jax.shard_map(shards, mesh=chip_mesh, in_specs=in_specs, out_specs=out_specs, check_vma=False)
```

```python
import jax
import jax.numpy as jnp
from jax import lax
from jax.sharding import PartitionSpec as P

HEADS = 24
KV_HEADS = 8
HEAD_DIM = 64
EXPERTS = 32
TOPK = 8
SHIFTS = 2
CAP = 40
CHUNKS = 2
TENSOR = ("chip", "core")


EPS = 1e-06
THETA = 10000.0


def from_behind(value, axis, steps):
    count = lax.axis_size(axis)
    first, last = (max(0, -steps), min(count, count - steps))
    return lax.ppermute(value, axis, [(source, source + steps) for source in range(first, last)])


def rms_norm(x, gain):
    values = x.astype(jnp.float32)
    mean_sq = jnp.mean(values * values, axis=-1, keepdims=True)
    return (values * lax.rsqrt(mean_sq + EPS) * gain).astype(jnp.bfloat16)


def rotary(x, positions):
    half = x.shape[-1] // 2
    freqs = THETA ** (-jnp.arange(half, dtype=jnp.float32) * 2.0 / x.shape[-1])
    angles = positions.astype(jnp.float32)[:, None] * freqs[None, :]
    cosine = jnp.concatenate([jnp.cos(angles), jnp.cos(angles)], axis=-1)[:, None, :]
    sine = jnp.concatenate([jnp.sin(angles), jnp.sin(angles)], axis=-1)[:, None, :]
    turned = jnp.concatenate([-x[..., half:], x[..., :half]], axis=-1)
    return x * cosine + turned * sine


def request_info(index, lengths):
    ends = jnp.cumsum(lengths, dtype=jnp.int32)
    before = ends[None, :] <= index[:, None]
    segment = jnp.sum(before.astype(jnp.int32), axis=1, dtype=jnp.int32)
    start = jnp.sum(jnp.where(before, lengths[None, :], 0), axis=1, dtype=jnp.int32)
    return (segment, index - start)


def merge_block(carry, scores, values, visible):
    best, total, acc = carry
    if visible is not None:
        scores = jnp.where(visible, scores, -1e30)
    newest = jnp.maximum(best, jnp.max(scores, axis=-1))
    probs = jnp.exp(scores - newest[..., None])
    if visible is not None:
        probs = jnp.where(visible, probs, 0.0)
    decay = jnp.exp(best - newest)
    total = total * decay + jnp.sum(probs, axis=-1)
    acc = acc * decay[..., None] + jnp.einsum(
        "tgrn,ngd->tgrd", probs.astype(jnp.bfloat16), values, preferred_element_type=jnp.float32
    )
    return (newest, total, acc)


def shards(
    tokens,
    attn_gain,
    qkv_weight,
    out_weight,
    prefix_cache,
    lengths,
    ffn_gain,
    expert_ids,
    gate_weights,
    expert_in,
    expert_out,
):
    rows = tokens.shape[1]
    model = tokens.shape[2]
    head_cols = HEADS * HEAD_DIM
    kv_cols = KV_HEADS * HEAD_DIM
    ratio = HEADS // KV_HEADS
    scale = 1.0 / HEAD_DIM**0.5
    lanes = lax.axis_size(TENSOR)
    prefix_len = prefix_cache.shape[1] * lanes
    own_lengths = lengths[0]
    inputs = tokens[0]
    normed = rms_norm(inputs, attn_gain)
    groups = lax.axis_size("dp")
    out_spread = jnp.broadcast_to(out_weight[None], (groups,) + out_weight.shape)
    full_out = lax.all_to_all(out_spread, "dp", 0, 0, tiled=True).reshape(groups * out_weight.shape[0], -1)
    spread = jnp.broadcast_to(normed[None], (groups, rows, model))
    group_rows = lax.all_to_all(spread, "dp", 0, 0, tiled=True).reshape(groups * rows, model)
    qkv_part = jnp.dot(group_rows, qkv_weight, preferred_element_type=jnp.float32).astype(jnp.bfloat16)
    qkv_back = lax.all_to_all(qkv_part.reshape(groups, rows, -1), "dp", 0, 0, tiled=True)
    qkv = jnp.transpose(qkv_back, (1, 0, 2)).reshape(rows, -1)
    lane = lax.axis_index(TENSOR)
    q_index = lane * rows + jnp.arange(rows, dtype=jnp.int32)
    q_segment, offset = request_info(q_index, own_lengths)
    positions = prefix_len + offset
    query = rotary(
        qkv[:, :head_cols].astype(jnp.float32).reshape(rows, HEADS, HEAD_DIM), positions
    ).astype(jnp.bfloat16)
    query = query.reshape(rows, KV_HEADS, ratio, HEAD_DIM)
    keys = rotary(
        qkv[:, head_cols : head_cols + kv_cols]
        .astype(jnp.float32)
        .reshape(rows, KV_HEADS, HEAD_DIM),
        positions,
    ).astype(jnp.bfloat16)
    local_pairs = jnp.stack([keys.reshape(rows, kv_cols), qkv[:, head_cols + kv_cols :]], axis=1)
    start_carry = (
        jnp.full((rows, KV_HEADS, ratio), -1e30, jnp.float32),
        jnp.zeros((rows, KV_HEADS, ratio), jnp.float32),
        jnp.zeros((rows, KV_HEADS, ratio, HEAD_DIM), jnp.float32),
    )
    window = local_pairs[None]
    for bit in range(SHIFTS):
        earlier = from_behind(window, TENSOR, 2**bit)
        window = jnp.concatenate([window, earlier], axis=0)
    depth = window.shape[0]
    k_index = (
        (lane - jnp.arange(depth, dtype=jnp.int32))[:, None] * rows
        + jnp.arange(rows, dtype=jnp.int32)[None, :]
    ).reshape(-1)
    k_segment, unused = request_info(k_index, own_lengths)
    visible = (
        (k_index[None, :] >= 0)
        & (k_index[None, :] <= q_index[:, None])
        & (k_segment[None, :] == q_segment[:, None])
    )
    suffix_pairs = window.reshape(depth * rows, 2, kv_cols)
    suffix_keys = suffix_pairs[:, 0].reshape(depth * rows, KV_HEADS, HEAD_DIM)
    suffix_values = suffix_pairs[:, 1].reshape(depth * rows, KV_HEADS, HEAD_DIM)
    scores = (
        jnp.einsum("tgrd,ngd->tgrn", query, suffix_keys, preferred_element_type=jnp.float32) * scale
    )
    carry = merge_block(start_carry, scores, suffix_values, visible[:, None, None, :])
    piece = lax.all_gather(prefix_cache[0], TENSOR, axis=0, tiled=True)
    piece, carry = lax.optimization_barrier((piece, carry))
    count = piece.shape[0]
    cached_keys = piece[:, 0].reshape(count, KV_HEADS, HEAD_DIM)
    cached_values = piece[:, 1].reshape(count, KV_HEADS, HEAD_DIM)
    scores = (
        jnp.einsum("tgrd,ngd->tgrn", query, cached_keys, preferred_element_type=jnp.float32) * scale
    )
    best, total, acc = merge_block(carry, scores, cached_values, None)
    attended = (acc / total[..., None]).astype(jnp.bfloat16).reshape(rows, head_cols)
    projected = jnp.dot(attended, full_out, preferred_element_type=jnp.float32)
    hidden_state = (inputs.astype(jnp.float32) + projected).astype(jnp.bfloat16)
    moe_input = rms_norm(hidden_state, ffn_gain)
    chips = lax.axis_size("chip")
    unit_ff = expert_in.shape[2] // 2
    own_ids = expert_ids[0]
    flat_ids = own_ids.reshape(-1)
    named = jnp.sum(
        (own_ids[:, :, None] == jnp.arange(EXPERTS, dtype=jnp.int32)[None, None, :]).astype(jnp.float32), axis=1
    )
    order = jnp.arange(rows, dtype=jnp.int32)
    below = (order[None, :] < order[:, None]).astype(jnp.bfloat16)
    earlier = jnp.dot(below, named.astype(jnp.bfloat16), preferred_element_type=jnp.float32)
    slots = jnp.take_along_axis(earlier, own_ids, axis=1).astype(jnp.int32).reshape(-1)
    part = CAP // CHUNKS
    target = (slots // part) * (chips * part) + flat_ids * part + slots % part
    row_of = jnp.repeat(jnp.arange(rows, dtype=jnp.int32), TOPK)
    source = jnp.full((chips * CAP,), rows, jnp.int32).at[target].set(row_of)
    padded_input = jnp.concatenate([moe_input, jnp.zeros((1, model), jnp.bfloat16)], axis=0)
    outgoing = padded_input[source].reshape(CHUNKS, chips, part, model)

    def unit(block):
        inner = jnp.dot(block.reshape(chips * part, model), expert_in[0], preferred_element_type=jnp.float32)
        activated = (jax.nn.silu(inner[:, :unit_ff]) * inner[:, unit_ff:]).astype(jnp.bfloat16)
        produced = jnp.dot(activated, expert_out[0], preferred_element_type=jnp.float32).astype(jnp.bfloat16)
        return produced.reshape(chips, part, model)

    pieces = []
    for chunk in range(CHUNKS):
        arrived = lax.all_to_all(outgoing[chunk], "chip", 0, 0, tiled=True)
        sibling = lax.ppermute(arrived, "core", [(0, 1), (1, 0)])
        own_part = unit(arrived)
        partner = lax.ppermute(unit(sibling), "core", [(0, 1), (1, 0)])
        summed = (own_part.astype(jnp.float32) + partner.astype(jnp.float32)).astype(jnp.bfloat16)
        pieces.append(lax.all_to_all(summed, "chip", 0, 0, tiled=True))
    returned = jnp.stack(pieces)
    picked = returned.reshape(chips * CAP, model)[target].reshape(rows, TOPK, model)
    combined = jnp.einsum("tk,tkd->td", gate_weights[0], picked.astype(jnp.float32))
    mixed = (hidden_state.astype(jnp.float32) + combined).astype(jnp.bfloat16)
    return (hidden_state[None], mixed[None])


def solution(mesh):
    groups, lanes = mesh.devices.shape
    chip_mesh = jax.sharding.Mesh(mesh.devices.reshape(groups, lanes // 2, 2), ("dp", "chip", "core"))
    in_specs = (
        P("dp", TENSOR, None),
        P(),
        P(None, "dp"),
        P("dp", None),
        P("dp", TENSOR, None, None),
        P("dp", None),
        P(),
        P("dp", TENSOR, None),
        P("dp", TENSOR, None),
        P(TENSOR, None, None),
        P(TENSOR, None, None),
    )
    out_specs = (P("dp", TENSOR, None), P("dp", TENSOR, None))
    return jax.shard_map(shards, mesh=chip_mesh, in_specs=in_specs, out_specs=out_specs, check_vma=False)
```

```python
import jax
import jax.numpy as jnp
from jax import lax
from jax.sharding import PartitionSpec as P

HEADS = 24
KV_HEADS = 8
HEAD_DIM = 64
EXPERTS = 32
TOPK = 8
SHIFTS = 2
CAP = 40
TENSOR = ("chip", "core")


EPS = 1e-06
THETA = 10000.0


def from_behind(value, axis, steps):
    count = lax.axis_size(axis)
    first, last = (max(0, -steps), min(count, count - steps))
    return lax.ppermute(value, axis, [(source, source + steps) for source in range(first, last)])


def rms_norm(x, gain):
    values = x.astype(jnp.float32)
    mean_sq = jnp.mean(values * values, axis=-1, keepdims=True)
    return (values * lax.rsqrt(mean_sq + EPS) * gain).astype(jnp.bfloat16)


def rotary(x, positions):
    half = x.shape[-1] // 2
    freqs = THETA ** (-jnp.arange(half, dtype=jnp.float32) * 2.0 / x.shape[-1])
    angles = positions.astype(jnp.float32)[:, None] * freqs[None, :]
    cosine = jnp.concatenate([jnp.cos(angles), jnp.cos(angles)], axis=-1)[:, None, :]
    sine = jnp.concatenate([jnp.sin(angles), jnp.sin(angles)], axis=-1)[:, None, :]
    turned = jnp.concatenate([-x[..., half:], x[..., :half]], axis=-1)
    return x * cosine + turned * sine


def request_info(index, lengths):
    ends = jnp.cumsum(lengths, dtype=jnp.int32)
    before = ends[None, :] <= index[:, None]
    segment = jnp.sum(before.astype(jnp.int32), axis=1, dtype=jnp.int32)
    start = jnp.sum(jnp.where(before, lengths[None, :], 0), axis=1, dtype=jnp.int32)
    return (segment, index - start)


def merge_block(carry, scores, values, visible):
    best, total, acc = carry
    if visible is not None:
        scores = jnp.where(visible, scores, -1e30)
    newest = jnp.maximum(best, jnp.max(scores, axis=-1))
    probs = jnp.exp(scores - newest[..., None])
    if visible is not None:
        probs = jnp.where(visible, probs, 0.0)
    decay = jnp.exp(best - newest)
    total = total * decay + jnp.sum(probs, axis=-1)
    acc = acc * decay[..., None] + jnp.einsum(
        "tgrn,ngd->tgrd", probs.astype(jnp.bfloat16), values, preferred_element_type=jnp.float32
    )
    return (newest, total, acc)


def shards(
    tokens,
    attn_gain,
    qkv_weight,
    out_weight,
    prefix_cache,
    lengths,
    ffn_gain,
    expert_ids,
    gate_weights,
    expert_in,
    expert_out,
):
    rows = tokens.shape[1]
    model = tokens.shape[2]
    head_cols = HEADS * HEAD_DIM
    kv_cols = KV_HEADS * HEAD_DIM
    ratio = HEADS // KV_HEADS
    scale = 1.0 / HEAD_DIM**0.5
    lanes = lax.axis_size(TENSOR)
    prefix_len = prefix_cache.shape[1] * lanes
    own_lengths = lengths[0]
    inputs = tokens[0]
    normed = rms_norm(inputs, attn_gain)
    groups = lax.axis_size("dp")
    out_spread = jnp.broadcast_to(out_weight[None], (groups,) + out_weight.shape)
    full_out = lax.all_to_all(out_spread, "dp", 0, 0, tiled=True).reshape(groups * out_weight.shape[0], -1)
    spread = jnp.broadcast_to(normed[None], (groups, rows, model))
    group_rows = lax.all_to_all(spread, "dp", 0, 0, tiled=True).reshape(groups * rows, model)
    qkv_part = jnp.dot(group_rows, qkv_weight, preferred_element_type=jnp.float32).astype(jnp.bfloat16)
    qkv_back = lax.all_to_all(qkv_part.reshape(groups, rows, -1), "dp", 0, 0, tiled=True)
    qkv = jnp.transpose(qkv_back, (1, 0, 2)).reshape(rows, -1)
    lane = lax.axis_index(TENSOR)
    q_index = lane * rows + jnp.arange(rows, dtype=jnp.int32)
    q_segment, offset = request_info(q_index, own_lengths)
    positions = prefix_len + offset
    query = rotary(
        qkv[:, :head_cols].astype(jnp.float32).reshape(rows, HEADS, HEAD_DIM), positions
    ).astype(jnp.bfloat16)
    query = query.reshape(rows, KV_HEADS, ratio, HEAD_DIM)
    keys = rotary(
        qkv[:, head_cols : head_cols + kv_cols]
        .astype(jnp.float32)
        .reshape(rows, KV_HEADS, HEAD_DIM),
        positions,
    ).astype(jnp.bfloat16)
    local_pairs = jnp.stack([keys.reshape(rows, kv_cols), qkv[:, head_cols + kv_cols :]], axis=1)
    start_carry = (
        jnp.full((rows, KV_HEADS, ratio), -1e30, jnp.float32),
        jnp.zeros((rows, KV_HEADS, ratio), jnp.float32),
        jnp.zeros((rows, KV_HEADS, ratio, HEAD_DIM), jnp.float32),
    )
    window = local_pairs[None]
    for bit in range(SHIFTS):
        earlier = from_behind(window, TENSOR, 2**bit)
        window = jnp.concatenate([window, earlier], axis=0)
    depth = window.shape[0]
    k_index = (
        (lane - jnp.arange(depth, dtype=jnp.int32))[:, None] * rows
        + jnp.arange(rows, dtype=jnp.int32)[None, :]
    ).reshape(-1)
    k_segment, unused = request_info(k_index, own_lengths)
    visible = (
        (k_index[None, :] >= 0)
        & (k_index[None, :] <= q_index[:, None])
        & (k_segment[None, :] == q_segment[:, None])
    )
    suffix_pairs = window.reshape(depth * rows, 2, kv_cols)
    suffix_keys = suffix_pairs[:, 0].reshape(depth * rows, KV_HEADS, HEAD_DIM)
    suffix_values = suffix_pairs[:, 1].reshape(depth * rows, KV_HEADS, HEAD_DIM)
    scores = (
        jnp.einsum("tgrd,ngd->tgrn", query, suffix_keys, preferred_element_type=jnp.float32) * scale
    )
    carry = merge_block(start_carry, scores, suffix_values, visible[:, None, None, :])
    piece = lax.all_gather(prefix_cache[0], TENSOR, axis=0, tiled=True)
    piece, carry = lax.optimization_barrier((piece, carry))
    count = piece.shape[0]
    cached_keys = piece[:, 0].reshape(count, KV_HEADS, HEAD_DIM)
    cached_values = piece[:, 1].reshape(count, KV_HEADS, HEAD_DIM)
    scores = (
        jnp.einsum("tgrd,ngd->tgrn", query, cached_keys, preferred_element_type=jnp.float32) * scale
    )
    best, total, acc = merge_block(carry, scores, cached_values, None)
    attended = (acc / total[..., None]).astype(jnp.bfloat16).reshape(rows, head_cols)
    projected = jnp.dot(attended, full_out, preferred_element_type=jnp.float32)
    hidden_state = (inputs.astype(jnp.float32) + projected).astype(jnp.bfloat16)
    moe_input = rms_norm(hidden_state, ffn_gain)
    chips = lax.axis_size("chip")
    unit_ff = expert_in.shape[2] // 2
    own_ids = expert_ids[0]
    picks = (own_ids[:, :, None] == jnp.arange(EXPERTS, dtype=jnp.int32)[None, None, :]).astype(jnp.float32)
    named = jnp.sum(picks, axis=1)
    gates = jnp.sum(picks * gate_weights[0][:, :, None], axis=1)
    order = jnp.arange(rows, dtype=jnp.int32)
    below = (order[None, :] < order[:, None]).astype(jnp.bfloat16)
    earlier = jnp.dot(below, named.astype(jnp.bfloat16), preferred_element_type=jnp.float32)
    at_slot = earlier[:, :, None] == jnp.arange(CAP, dtype=jnp.float32)[None, None, :]
    routes = jnp.where(at_slot, named[:, :, None], 0.0).reshape(rows, chips * CAP)
    weights = jnp.where(at_slot, gates[:, :, None], 0.0).reshape(rows, chips * CAP)
    outgoing = jnp.dot(routes.astype(jnp.bfloat16).T, moe_input, preferred_element_type=jnp.float32)
    outgoing = outgoing.astype(jnp.bfloat16).reshape(chips, CAP, model)
    arrived = lax.all_to_all(outgoing, "chip", 0, 0, tiled=True)
    sibling = lax.ppermute(arrived, "core", [(0, 1), (1, 0)])

    def unit(block):
        inner = jnp.dot(block.reshape(chips * CAP, model), expert_in[0], preferred_element_type=jnp.float32)
        activated = (jax.nn.silu(inner[:, :unit_ff]) * inner[:, unit_ff:]).astype(jnp.bfloat16)
        produced = jnp.dot(activated, expert_out[0], preferred_element_type=jnp.float32).astype(jnp.bfloat16)
        return produced.reshape(chips, CAP, model)

    own_part = unit(arrived)
    partner = lax.ppermute(unit(sibling), "core", [(0, 1), (1, 0)])
    summed = (own_part.astype(jnp.float32) + partner.astype(jnp.float32)).astype(jnp.bfloat16)
    returned = lax.all_to_all(summed, "chip", 0, 0, tiled=True)
    returned = returned.reshape(chips * CAP, model)
    weights_hi = weights.astype(jnp.bfloat16)
    weights_lo = (weights - weights_hi.astype(jnp.float32)).astype(jnp.bfloat16)
    combined = jnp.dot(weights_hi, returned, preferred_element_type=jnp.float32) + jnp.dot(
        weights_lo, returned, preferred_element_type=jnp.float32
    )
    mixed = (hidden_state.astype(jnp.float32) + combined).astype(jnp.bfloat16)
    return (hidden_state[None], mixed[None])


def solution(mesh):
    groups, lanes = mesh.devices.shape
    chip_mesh = jax.sharding.Mesh(mesh.devices.reshape(groups, lanes // 2, 2), ("dp", "chip", "core"))
    in_specs = (
        P("dp", TENSOR, None),
        P(),
        P(None, "dp"),
        P("dp", None),
        P("dp", TENSOR, None, None),
        P("dp", None),
        P(),
        P("dp", TENSOR, None),
        P("dp", TENSOR, None),
        P(TENSOR, None, None),
        P(TENSOR, None, None),
    )
    out_specs = (P("dp", TENSOR, None), P("dp", TENSOR, None))
    return jax.shard_map(shards, mesh=chip_mesh, in_specs=in_specs, out_specs=out_specs, check_vma=False)
```

```python
import jax
import jax.numpy as jnp
from jax import lax
from jax.sharding import PartitionSpec as P

HEADS = 24
KV_HEADS = 8
HEAD_DIM = 64
EXPERTS = 32
TOPK = 8
SHIFTS = 2
CAP = 40
TENSOR = ("chip", "core")


EPS = 1e-06
THETA = 10000.0


def from_behind(value, axis, steps):
    count = lax.axis_size(axis)
    first, last = (max(0, -steps), min(count, count - steps))
    return lax.ppermute(value, axis, [(source, source + steps) for source in range(first, last)])


def rms_norm(x, gain):
    values = x.astype(jnp.float32)
    mean_sq = jnp.mean(values * values, axis=-1, keepdims=True)
    return (values * lax.rsqrt(mean_sq + EPS) * gain).astype(jnp.bfloat16)


def rotary(x, positions):
    half = x.shape[-1] // 2
    freqs = THETA ** (-jnp.arange(half, dtype=jnp.float32) * 2.0 / x.shape[-1])
    angles = positions.astype(jnp.float32)[:, None] * freqs[None, :]
    cosine = jnp.concatenate([jnp.cos(angles), jnp.cos(angles)], axis=-1)[:, None, :]
    sine = jnp.concatenate([jnp.sin(angles), jnp.sin(angles)], axis=-1)[:, None, :]
    turned = jnp.concatenate([-x[..., half:], x[..., :half]], axis=-1)
    return x * cosine + turned * sine


def request_info(index, lengths):
    ends = jnp.cumsum(lengths, dtype=jnp.int32)
    before = ends[None, :] <= index[:, None]
    segment = jnp.sum(before.astype(jnp.int32), axis=1, dtype=jnp.int32)
    start = jnp.sum(jnp.where(before, lengths[None, :], 0), axis=1, dtype=jnp.int32)
    return (segment, index - start)


def merge_block(carry, scores, values, visible):
    best, total, acc = carry
    if visible is not None:
        scores = jnp.where(visible, scores, -1e30)
    newest = jnp.maximum(best, jnp.max(scores, axis=-1))
    probs = jnp.exp(scores - newest[..., None])
    if visible is not None:
        probs = jnp.where(visible, probs, 0.0)
    decay = jnp.exp(best - newest)
    total = total * decay + jnp.sum(probs, axis=-1)
    acc = acc * decay[..., None] + jnp.einsum(
        "tgrn,ngd->tgrd", probs.astype(jnp.bfloat16), values, preferred_element_type=jnp.float32
    )
    return (newest, total, acc)


def shards(
    tokens,
    attn_gain,
    qkv_weight,
    out_weight,
    prefix_cache,
    lengths,
    ffn_gain,
    expert_ids,
    gate_weights,
    expert_in,
    expert_out,
):
    rows = tokens.shape[1]
    model = tokens.shape[2]
    head_cols = HEADS * HEAD_DIM
    kv_cols = KV_HEADS * HEAD_DIM
    ratio = HEADS // KV_HEADS
    scale = 1.0 / HEAD_DIM**0.5
    lanes = lax.axis_size(TENSOR)
    prefix_len = prefix_cache.shape[1] * lanes
    own_lengths = lengths[0]
    inputs = tokens[0]
    normed = rms_norm(inputs, attn_gain)
    groups = lax.axis_size("dp")
    ring = lax.axis_index("dp")
    out_pieces = [out_weight] + [
        lax.ppermute(out_weight, "dp", [(source, (source + step) % groups) for source in range(groups)])
        for step in range(1, groups)
    ]
    spread = jnp.broadcast_to(normed[None], (groups, rows, model))
    group_rows = lax.all_to_all(spread, "dp", 0, 0, tiled=True).reshape(groups * rows, model)
    qkv_part = jnp.dot(group_rows, qkv_weight, preferred_element_type=jnp.float32).astype(jnp.bfloat16)
    qkv_back = lax.all_to_all(qkv_part.reshape(groups, rows, -1), "dp", 0, 0, tiled=True)
    qkv = jnp.transpose(qkv_back, (1, 0, 2)).reshape(rows, -1)
    lane = lax.axis_index(TENSOR)
    q_index = lane * rows + jnp.arange(rows, dtype=jnp.int32)
    q_segment, offset = request_info(q_index, own_lengths)
    positions = prefix_len + offset
    query = rotary(
        qkv[:, :head_cols].astype(jnp.float32).reshape(rows, HEADS, HEAD_DIM), positions
    ).astype(jnp.bfloat16)
    query = query.reshape(rows, KV_HEADS, ratio, HEAD_DIM)
    keys = rotary(
        qkv[:, head_cols : head_cols + kv_cols]
        .astype(jnp.float32)
        .reshape(rows, KV_HEADS, HEAD_DIM),
        positions,
    ).astype(jnp.bfloat16)
    local_pairs = jnp.stack([keys.reshape(rows, kv_cols), qkv[:, head_cols + kv_cols :]], axis=1)
    start_carry = (
        jnp.full((rows, KV_HEADS, ratio), -1e30, jnp.float32),
        jnp.zeros((rows, KV_HEADS, ratio), jnp.float32),
        jnp.zeros((rows, KV_HEADS, ratio, HEAD_DIM), jnp.float32),
    )
    window = local_pairs[None]
    for bit in range(SHIFTS):
        earlier = from_behind(window, TENSOR, 2**bit)
        window = jnp.concatenate([window, earlier], axis=0)
    depth = window.shape[0]
    k_index = (
        (lane - jnp.arange(depth, dtype=jnp.int32))[:, None] * rows
        + jnp.arange(rows, dtype=jnp.int32)[None, :]
    ).reshape(-1)
    k_segment, unused = request_info(k_index, own_lengths)
    visible = (
        (k_index[None, :] >= 0)
        & (k_index[None, :] <= q_index[:, None])
        & (k_segment[None, :] == q_segment[:, None])
    )
    suffix_pairs = window.reshape(depth * rows, 2, kv_cols)
    suffix_keys = suffix_pairs[:, 0].reshape(depth * rows, KV_HEADS, HEAD_DIM)
    suffix_values = suffix_pairs[:, 1].reshape(depth * rows, KV_HEADS, HEAD_DIM)
    scores = (
        jnp.einsum("tgrd,ngd->tgrn", query, suffix_keys, preferred_element_type=jnp.float32) * scale
    )
    carry = merge_block(start_carry, scores, suffix_values, visible[:, None, None, :])
    piece = lax.all_gather(prefix_cache[0], TENSOR, axis=0, tiled=True)
    piece, carry = lax.optimization_barrier((piece, carry))
    count = piece.shape[0]
    cached_keys = piece[:, 0].reshape(count, KV_HEADS, HEAD_DIM)
    cached_values = piece[:, 1].reshape(count, KV_HEADS, HEAD_DIM)
    scores = (
        jnp.einsum("tgrd,ngd->tgrn", query, cached_keys, preferred_element_type=jnp.float32) * scale
    )
    best, total, acc = merge_block(carry, scores, cached_values, None)
    attended = (acc / total[..., None]).astype(jnp.bfloat16).reshape(rows, head_cols)
    band = out_weight.shape[0]
    projected = None
    for step, piece_w in enumerate(out_pieces):
        first = ((ring - step) % groups) * band
        part_in = lax.dynamic_slice_in_dim(attended, first, band, axis=1)
        term = jnp.dot(part_in, piece_w, preferred_element_type=jnp.float32)
        projected = term if projected is None else projected + term
    hidden_state = (inputs.astype(jnp.float32) + projected).astype(jnp.bfloat16)
    moe_input = rms_norm(hidden_state, ffn_gain)
    chips = lax.axis_size("chip")
    unit_ff = expert_in.shape[2] // 2
    own_ids = expert_ids[0]
    picks = (own_ids[:, :, None] == jnp.arange(EXPERTS, dtype=jnp.int32)[None, None, :]).astype(jnp.float32)
    named = jnp.sum(picks, axis=1)
    gates = jnp.sum(picks * gate_weights[0][:, :, None], axis=1)
    order = jnp.arange(rows, dtype=jnp.int32)
    below = (order[None, :] < order[:, None]).astype(jnp.bfloat16)
    earlier = jnp.dot(below, named.astype(jnp.bfloat16), preferred_element_type=jnp.float32)
    at_slot = earlier[:, :, None] == jnp.arange(CAP, dtype=jnp.float32)[None, None, :]
    routes = jnp.where(at_slot, named[:, :, None], 0.0).reshape(rows, chips * CAP)
    weights = jnp.where(at_slot, gates[:, :, None], 0.0).reshape(rows, chips * CAP)
    outgoing = jnp.dot(routes.astype(jnp.bfloat16).T, moe_input, preferred_element_type=jnp.float32)
    outgoing = outgoing.astype(jnp.bfloat16).reshape(chips, CAP, model)
    arrived = lax.all_to_all(outgoing, "chip", 0, 0, tiled=True)
    sibling = lax.ppermute(arrived, "core", [(0, 1), (1, 0)])

    def unit(block):
        inner = jnp.dot(block.reshape(chips * CAP, model), expert_in[0], preferred_element_type=jnp.float32)
        activated = (jax.nn.silu(inner[:, :unit_ff]) * inner[:, unit_ff:]).astype(jnp.bfloat16)
        produced = jnp.dot(activated, expert_out[0], preferred_element_type=jnp.float32).astype(jnp.bfloat16)
        return produced.reshape(chips, CAP, model)

    own_part = unit(arrived)
    partner = lax.ppermute(unit(sibling), "core", [(0, 1), (1, 0)])
    summed = (own_part.astype(jnp.float32) + partner.astype(jnp.float32)).astype(jnp.bfloat16)
    returned = lax.all_to_all(summed, "chip", 0, 0, tiled=True)
    returned = returned.reshape(chips * CAP, model)
    weights_hi = weights.astype(jnp.bfloat16)
    weights_lo = (weights - weights_hi.astype(jnp.float32)).astype(jnp.bfloat16)
    combined = jnp.dot(weights_hi, returned, preferred_element_type=jnp.float32) + jnp.dot(
        weights_lo, returned, preferred_element_type=jnp.float32
    )
    mixed = (hidden_state.astype(jnp.float32) + combined).astype(jnp.bfloat16)
    return (hidden_state[None], mixed[None])


def solution(mesh):
    groups, lanes = mesh.devices.shape
    chip_mesh = jax.sharding.Mesh(mesh.devices.reshape(groups, lanes // 2, 2), ("dp", "chip", "core"))
    in_specs = (
        P("dp", TENSOR, None),
        P(),
        P(None, "dp"),
        P("dp", None),
        P("dp", TENSOR, None, None),
        P("dp", None),
        P(),
        P("dp", TENSOR, None),
        P("dp", TENSOR, None),
        P(TENSOR, None, None),
        P(TENSOR, None, None),
    )
    out_specs = (P("dp", TENSOR, None), P("dp", TENSOR, None))
    return jax.shard_map(shards, mesh=chip_mesh, in_specs=in_specs, out_specs=out_specs, check_vma=False)
```

```python
import jax
import jax.numpy as jnp
from jax import lax
from jax.sharding import PartitionSpec as P

HEADS = 24
KV_HEADS = 8
HEAD_DIM = 64
EXPERTS = 32
TOPK = 8
SHIFTS = 2
CAP = 40
TENSOR = ("chip", "core")


EPS = 1e-06
THETA = 10000.0


def from_behind(value, axis, steps):
    count = lax.axis_size(axis)
    first, last = (max(0, -steps), min(count, count - steps))
    return lax.ppermute(value, axis, [(source, source + steps) for source in range(first, last)])


def rms_norm(x, gain):
    values = x.astype(jnp.float32)
    mean_sq = jnp.mean(values * values, axis=-1, keepdims=True)
    return (values * lax.rsqrt(mean_sq + EPS) * gain).astype(jnp.bfloat16)


def rotary(x, positions):
    half = x.shape[-1] // 2
    freqs = THETA ** (-jnp.arange(half, dtype=jnp.float32) * 2.0 / x.shape[-1])
    angles = positions.astype(jnp.float32)[:, None] * freqs[None, :]
    cosine = jnp.concatenate([jnp.cos(angles), jnp.cos(angles)], axis=-1)[:, None, :]
    sine = jnp.concatenate([jnp.sin(angles), jnp.sin(angles)], axis=-1)[:, None, :]
    turned = jnp.concatenate([-x[..., half:], x[..., :half]], axis=-1)
    return x * cosine + turned * sine


def request_info(index, lengths):
    ends = jnp.cumsum(lengths, dtype=jnp.int32)
    before = ends[None, :] <= index[:, None]
    segment = jnp.sum(before.astype(jnp.int32), axis=1, dtype=jnp.int32)
    start = jnp.sum(jnp.where(before, lengths[None, :], 0), axis=1, dtype=jnp.int32)
    return (segment, index - start)


def merge_block(carry, scores, values, visible):
    best, total, acc = carry
    if visible is not None:
        scores = jnp.where(visible, scores, -1e30)
    newest = jnp.maximum(best, jnp.max(scores, axis=-1))
    probs = jnp.exp(scores - newest[..., None])
    if visible is not None:
        probs = jnp.where(visible, probs, 0.0)
    decay = jnp.exp(best - newest)
    total = total * decay + jnp.sum(probs, axis=-1)
    acc = acc * decay[..., None] + jnp.einsum(
        "tgrn,ngd->tgrd", probs.astype(jnp.bfloat16), values, preferred_element_type=jnp.float32
    )
    return (newest, total, acc)


def shards(
    tokens,
    attn_gain,
    qkv_weight,
    out_weight,
    prefix_cache,
    lengths,
    ffn_gain,
    expert_ids,
    gate_weights,
    expert_in,
    expert_out,
):
    rows = tokens.shape[1]
    model = tokens.shape[2]
    head_cols = HEADS * HEAD_DIM
    kv_cols = KV_HEADS * HEAD_DIM
    ratio = HEADS // KV_HEADS
    scale = 1.0 / HEAD_DIM**0.5
    lanes = lax.axis_size(TENSOR)
    prefix_len = prefix_cache.shape[1] * lanes
    own_lengths = lengths[0]
    inputs = tokens[0]
    normed = rms_norm(inputs, attn_gain)
    groups = lax.axis_size("dp")
    spread = jnp.broadcast_to(normed[None], (groups, rows, model))
    group_rows = lax.all_to_all(spread, "dp", 0, 0, tiled=True).reshape(groups * rows, model)
    qkv_part = jnp.dot(group_rows, qkv_weight, preferred_element_type=jnp.float32).astype(jnp.bfloat16)
    qkv_back = lax.all_to_all(qkv_part.reshape(groups, rows, -1), "dp", 0, 0, tiled=True)
    qkv = jnp.transpose(qkv_back, (1, 0, 2)).reshape(rows, -1)
    lane = lax.axis_index(TENSOR)
    q_index = lane * rows + jnp.arange(rows, dtype=jnp.int32)
    q_segment, offset = request_info(q_index, own_lengths)
    positions = prefix_len + offset
    query = rotary(
        qkv[:, :head_cols].astype(jnp.float32).reshape(rows, HEADS, HEAD_DIM), positions
    ).astype(jnp.bfloat16)
    query = query.reshape(rows, KV_HEADS, ratio, HEAD_DIM)
    keys = rotary(
        qkv[:, head_cols : head_cols + kv_cols]
        .astype(jnp.float32)
        .reshape(rows, KV_HEADS, HEAD_DIM),
        positions,
    ).astype(jnp.bfloat16)
    local_pairs = jnp.stack([keys.reshape(rows, kv_cols), qkv[:, head_cols + kv_cols :]], axis=1)
    start_carry = (
        jnp.full((rows, KV_HEADS, ratio), -1e30, jnp.float32),
        jnp.zeros((rows, KV_HEADS, ratio), jnp.float32),
        jnp.zeros((rows, KV_HEADS, ratio, HEAD_DIM), jnp.float32),
    )
    window = local_pairs[None]
    for bit in range(SHIFTS):
        earlier = from_behind(window, TENSOR, 2**bit)
        window = jnp.concatenate([window, earlier], axis=0)
    out_spread = jnp.broadcast_to(out_weight[None], (groups,) + out_weight.shape)
    out_spread, window = lax.optimization_barrier((out_spread, window))
    full_out = lax.all_to_all(out_spread, "dp", 0, 0, tiled=True).reshape(groups * out_weight.shape[0], -1)
    depth = window.shape[0]
    k_index = (
        (lane - jnp.arange(depth, dtype=jnp.int32))[:, None] * rows
        + jnp.arange(rows, dtype=jnp.int32)[None, :]
    ).reshape(-1)
    k_segment, unused = request_info(k_index, own_lengths)
    visible = (
        (k_index[None, :] >= 0)
        & (k_index[None, :] <= q_index[:, None])
        & (k_segment[None, :] == q_segment[:, None])
    )
    suffix_pairs = window.reshape(depth * rows, 2, kv_cols)
    suffix_keys = suffix_pairs[:, 0].reshape(depth * rows, KV_HEADS, HEAD_DIM)
    suffix_values = suffix_pairs[:, 1].reshape(depth * rows, KV_HEADS, HEAD_DIM)
    scores = (
        jnp.einsum("tgrd,ngd->tgrn", query, suffix_keys, preferred_element_type=jnp.float32) * scale
    )
    carry = merge_block(start_carry, scores, suffix_values, visible[:, None, None, :])
    piece = lax.all_gather(prefix_cache[0], TENSOR, axis=0, tiled=True)
    piece, carry = lax.optimization_barrier((piece, carry))
    count = piece.shape[0]
    cached_keys = piece[:, 0].reshape(count, KV_HEADS, HEAD_DIM)
    cached_values = piece[:, 1].reshape(count, KV_HEADS, HEAD_DIM)
    scores = (
        jnp.einsum("tgrd,ngd->tgrn", query, cached_keys, preferred_element_type=jnp.float32) * scale
    )
    best, total, acc = merge_block(carry, scores, cached_values, None)
    attended = (acc / total[..., None]).astype(jnp.bfloat16).reshape(rows, head_cols)
    projected = jnp.dot(attended, full_out, preferred_element_type=jnp.float32)
    hidden_state = (inputs.astype(jnp.float32) + projected).astype(jnp.bfloat16)
    moe_input = rms_norm(hidden_state, ffn_gain)
    chips = lax.axis_size("chip")
    unit_ff = expert_in.shape[2] // 2
    own_ids = expert_ids[0]
    picks = (own_ids[:, :, None] == jnp.arange(EXPERTS, dtype=jnp.int32)[None, None, :]).astype(jnp.float32)
    named = jnp.sum(picks, axis=1)
    gates = jnp.sum(picks * gate_weights[0][:, :, None], axis=1)
    order = jnp.arange(rows, dtype=jnp.int32)
    below = (order[None, :] < order[:, None]).astype(jnp.bfloat16)
    earlier = jnp.dot(below, named.astype(jnp.bfloat16), preferred_element_type=jnp.float32)
    at_slot = earlier[:, :, None] == jnp.arange(CAP, dtype=jnp.float32)[None, None, :]
    routes = jnp.where(at_slot, named[:, :, None], 0.0).reshape(rows, chips * CAP)
    weights = jnp.where(at_slot, gates[:, :, None], 0.0).reshape(rows, chips * CAP)
    outgoing = jnp.dot(routes.astype(jnp.bfloat16).T, moe_input, preferred_element_type=jnp.float32)
    outgoing = outgoing.astype(jnp.bfloat16).reshape(chips, CAP, model)
    arrived = lax.all_to_all(outgoing, "chip", 0, 0, tiled=True)
    sibling = lax.ppermute(arrived, "core", [(0, 1), (1, 0)])

    def unit(block):
        inner = jnp.dot(block.reshape(chips * CAP, model), expert_in[0], preferred_element_type=jnp.float32)
        activated = (jax.nn.silu(inner[:, :unit_ff]) * inner[:, unit_ff:]).astype(jnp.bfloat16)
        produced = jnp.dot(activated, expert_out[0], preferred_element_type=jnp.float32).astype(jnp.bfloat16)
        return produced.reshape(chips, CAP, model)

    own_part = unit(arrived)
    partner = lax.ppermute(unit(sibling), "core", [(0, 1), (1, 0)])
    summed = (own_part.astype(jnp.float32) + partner.astype(jnp.float32)).astype(jnp.bfloat16)
    returned = lax.all_to_all(summed, "chip", 0, 0, tiled=True)
    returned = returned.reshape(chips * CAP, model)
    weights_hi = weights.astype(jnp.bfloat16)
    weights_lo = (weights - weights_hi.astype(jnp.float32)).astype(jnp.bfloat16)
    combined = jnp.dot(weights_hi, returned, preferred_element_type=jnp.float32) + jnp.dot(
        weights_lo, returned, preferred_element_type=jnp.float32
    )
    mixed = (hidden_state.astype(jnp.float32) + combined).astype(jnp.bfloat16)
    return (hidden_state[None], mixed[None])


def solution(mesh):
    groups, lanes = mesh.devices.shape
    chip_mesh = jax.sharding.Mesh(mesh.devices.reshape(groups, lanes // 2, 2), ("dp", "chip", "core"))
    in_specs = (
        P("dp", TENSOR, None),
        P(),
        P(None, "dp"),
        P("dp", None),
        P("dp", TENSOR, None, None),
        P("dp", None),
        P(),
        P("dp", TENSOR, None),
        P("dp", TENSOR, None),
        P(TENSOR, None, None),
        P(TENSOR, None, None),
    )
    out_specs = (P("dp", TENSOR, None), P("dp", TENSOR, None))
    return jax.shard_map(shards, mesh=chip_mesh, in_specs=in_specs, out_specs=out_specs, check_vma=False)
```

```python
import jax
import jax.numpy as jnp
from jax import lax
from jax.experimental import pallas as pl
from jax.sharding import PartitionSpec as P

HEADS = 24
KV_HEADS = 8
HEAD_DIM = 64
EXPERTS = 32
TOPK = 8
SHIFTS = 2
CAP = 40
TENSOR = ("chip", "core")


EPS = 1e-06
THETA = 10000.0


def from_behind(value, axis, steps):
    count = lax.axis_size(axis)
    first, last = (max(0, -steps), min(count, count - steps))
    return lax.ppermute(value, axis, [(source, source + steps) for source in range(first, last)])


def unit_kernel(x_ref, win_ref, wout_ref, o_ref):
    inner = jnp.dot(x_ref[...], win_ref[...], preferred_element_type=jnp.float32)
    half = inner.shape[1] // 2
    gate = inner[:, :half]
    act = (gate / (1.0 + jnp.exp(-gate)) * inner[:, half:]).astype(jnp.bfloat16)
    o_ref[...] = jnp.dot(act, wout_ref[...], preferred_element_type=jnp.float32).astype(o_ref.dtype)


def unit_call(x, w_in, w_out, tile=320):
    n, d = x.shape
    f = w_in.shape[1]
    return pl.pallas_call(
        unit_kernel,
        grid=(n // tile,),
        in_specs=[
            pl.BlockSpec((tile, d), lambda i: (i, 0)),
            pl.BlockSpec((d, f), lambda i: (0, 0)),
            pl.BlockSpec((f // 2, d), lambda i: (0, 0)),
        ],
        out_specs=pl.BlockSpec((tile, d), lambda i: (i, 0)),
        out_shape=jax.ShapeDtypeStruct((n, d), jnp.bfloat16),
    )(x, w_in, w_out)


def rms_norm(x, gain):
    values = x.astype(jnp.float32)
    mean_sq = jnp.mean(values * values, axis=-1, keepdims=True)
    return (values * lax.rsqrt(mean_sq + EPS) * gain).astype(jnp.bfloat16)


def rotary(x, positions):
    half = x.shape[-1] // 2
    freqs = THETA ** (-jnp.arange(half, dtype=jnp.float32) * 2.0 / x.shape[-1])
    angles = positions.astype(jnp.float32)[:, None] * freqs[None, :]
    cosine = jnp.concatenate([jnp.cos(angles), jnp.cos(angles)], axis=-1)[:, None, :]
    sine = jnp.concatenate([jnp.sin(angles), jnp.sin(angles)], axis=-1)[:, None, :]
    turned = jnp.concatenate([-x[..., half:], x[..., :half]], axis=-1)
    return x * cosine + turned * sine


def request_info(index, lengths):
    ends = jnp.cumsum(lengths, dtype=jnp.int32)
    before = ends[None, :] <= index[:, None]
    segment = jnp.sum(before.astype(jnp.int32), axis=1, dtype=jnp.int32)
    start = jnp.sum(jnp.where(before, lengths[None, :], 0), axis=1, dtype=jnp.int32)
    return (segment, index - start)


def merge_block(carry, scores, values, visible):
    best, total, acc = carry
    if visible is not None:
        scores = jnp.where(visible, scores, -1e30)
    newest = jnp.maximum(best, jnp.max(scores, axis=-1))
    probs = jnp.exp(scores - newest[..., None])
    if visible is not None:
        probs = jnp.where(visible, probs, 0.0)
    decay = jnp.exp(best - newest)
    total = total * decay + jnp.sum(probs, axis=-1)
    acc = acc * decay[..., None] + jnp.einsum(
        "tgrn,ngd->tgrd", probs.astype(jnp.bfloat16), values, preferred_element_type=jnp.float32
    )
    return (newest, total, acc)


def shards(
    tokens,
    attn_gain,
    qkv_weight,
    out_weight,
    prefix_cache,
    lengths,
    ffn_gain,
    expert_ids,
    gate_weights,
    expert_in,
    expert_out,
):
    rows = tokens.shape[1]
    model = tokens.shape[2]
    head_cols = HEADS * HEAD_DIM
    kv_cols = KV_HEADS * HEAD_DIM
    ratio = HEADS // KV_HEADS
    scale = 1.0 / HEAD_DIM**0.5
    lanes = lax.axis_size(TENSOR)
    prefix_len = prefix_cache.shape[1] * lanes
    own_lengths = lengths[0]
    inputs = tokens[0]
    normed = rms_norm(inputs, attn_gain)
    groups = lax.axis_size("dp")
    out_spread = jnp.broadcast_to(out_weight[None], (groups,) + out_weight.shape)
    full_out = lax.all_to_all(out_spread, "dp", 0, 0, tiled=True).reshape(groups * out_weight.shape[0], -1)
    spread = jnp.broadcast_to(normed[None], (groups, rows, model))
    group_rows = lax.all_to_all(spread, "dp", 0, 0, tiled=True).reshape(groups * rows, model)
    qkv_part = jnp.dot(group_rows, qkv_weight, preferred_element_type=jnp.float32).astype(jnp.bfloat16)
    qkv_back = lax.all_to_all(qkv_part.reshape(groups, rows, -1), "dp", 0, 0, tiled=True)
    qkv = jnp.transpose(qkv_back, (1, 0, 2)).reshape(rows, -1)
    lane = lax.axis_index(TENSOR)
    q_index = lane * rows + jnp.arange(rows, dtype=jnp.int32)
    q_segment, offset = request_info(q_index, own_lengths)
    positions = prefix_len + offset
    query = rotary(
        qkv[:, :head_cols].astype(jnp.float32).reshape(rows, HEADS, HEAD_DIM), positions
    ).astype(jnp.bfloat16)
    query = query.reshape(rows, KV_HEADS, ratio, HEAD_DIM)
    keys = rotary(
        qkv[:, head_cols : head_cols + kv_cols]
        .astype(jnp.float32)
        .reshape(rows, KV_HEADS, HEAD_DIM),
        positions,
    ).astype(jnp.bfloat16)
    local_pairs = jnp.stack([keys.reshape(rows, kv_cols), qkv[:, head_cols + kv_cols :]], axis=1)
    start_carry = (
        jnp.full((rows, KV_HEADS, ratio), -1e30, jnp.float32),
        jnp.zeros((rows, KV_HEADS, ratio), jnp.float32),
        jnp.zeros((rows, KV_HEADS, ratio, HEAD_DIM), jnp.float32),
    )
    window = local_pairs[None]
    for bit in range(SHIFTS):
        earlier = from_behind(window, TENSOR, 2**bit)
        window = jnp.concatenate([window, earlier], axis=0)
    depth = window.shape[0]
    k_index = (
        (lane - jnp.arange(depth, dtype=jnp.int32))[:, None] * rows
        + jnp.arange(rows, dtype=jnp.int32)[None, :]
    ).reshape(-1)
    k_segment, unused = request_info(k_index, own_lengths)
    visible = (
        (k_index[None, :] >= 0)
        & (k_index[None, :] <= q_index[:, None])
        & (k_segment[None, :] == q_segment[:, None])
    )
    suffix_pairs = window.reshape(depth * rows, 2, kv_cols)
    suffix_keys = suffix_pairs[:, 0].reshape(depth * rows, KV_HEADS, HEAD_DIM)
    suffix_values = suffix_pairs[:, 1].reshape(depth * rows, KV_HEADS, HEAD_DIM)
    scores = (
        jnp.einsum("tgrd,ngd->tgrn", query, suffix_keys, preferred_element_type=jnp.float32) * scale
    )
    carry = merge_block(start_carry, scores, suffix_values, visible[:, None, None, :])
    piece = lax.all_gather(prefix_cache[0], TENSOR, axis=0, tiled=True)
    piece, carry = lax.optimization_barrier((piece, carry))
    count = piece.shape[0]
    cached_keys = piece[:, 0].reshape(count, KV_HEADS, HEAD_DIM)
    cached_values = piece[:, 1].reshape(count, KV_HEADS, HEAD_DIM)
    scores = (
        jnp.einsum("tgrd,ngd->tgrn", query, cached_keys, preferred_element_type=jnp.float32) * scale
    )
    best, total, acc = merge_block(carry, scores, cached_values, None)
    attended = (acc / total[..., None]).astype(jnp.bfloat16).reshape(rows, head_cols)
    projected = jnp.dot(attended, full_out, preferred_element_type=jnp.float32)
    hidden_state = (inputs.astype(jnp.float32) + projected).astype(jnp.bfloat16)
    moe_input = rms_norm(hidden_state, ffn_gain)
    chips = lax.axis_size("chip")
    unit_ff = expert_in.shape[2] // 2
    own_ids = expert_ids[0]
    picks = (own_ids[:, :, None] == jnp.arange(EXPERTS, dtype=jnp.int32)[None, None, :]).astype(jnp.float32)
    named = jnp.sum(picks, axis=1)
    gates = jnp.sum(picks * gate_weights[0][:, :, None], axis=1)
    order = jnp.arange(rows, dtype=jnp.int32)
    below = (order[None, :] < order[:, None]).astype(jnp.bfloat16)
    earlier = jnp.dot(below, named.astype(jnp.bfloat16), preferred_element_type=jnp.float32)
    at_slot = earlier[:, :, None] == jnp.arange(CAP, dtype=jnp.float32)[None, None, :]
    routes = jnp.where(at_slot, named[:, :, None], 0.0).reshape(rows, chips * CAP)
    weights = jnp.where(at_slot, gates[:, :, None], 0.0).reshape(rows, chips * CAP)
    outgoing = jnp.dot(routes.astype(jnp.bfloat16).T, moe_input, preferred_element_type=jnp.float32)
    outgoing = outgoing.astype(jnp.bfloat16).reshape(chips, CAP, model)
    arrived = lax.all_to_all(outgoing, "chip", 0, 0, tiled=True)
    sibling = lax.ppermute(arrived, "core", [(0, 1), (1, 0)])

    def unit(block):
        produced = unit_call(block.reshape(chips * CAP, model), expert_in[0], expert_out[0])
        return produced.reshape(chips, CAP, model)

    own_part = unit(arrived)
    partner = lax.ppermute(unit(sibling), "core", [(0, 1), (1, 0)])
    summed = (own_part.astype(jnp.float32) + partner.astype(jnp.float32)).astype(jnp.bfloat16)
    returned = lax.all_to_all(summed, "chip", 0, 0, tiled=True)
    returned = returned.reshape(chips * CAP, model)
    weights_hi = weights.astype(jnp.bfloat16)
    weights_lo = (weights - weights_hi.astype(jnp.float32)).astype(jnp.bfloat16)
    combined = jnp.dot(weights_hi, returned, preferred_element_type=jnp.float32) + jnp.dot(
        weights_lo, returned, preferred_element_type=jnp.float32
    )
    mixed = (hidden_state.astype(jnp.float32) + combined).astype(jnp.bfloat16)
    return (hidden_state[None], mixed[None])


def solution(mesh):
    groups, lanes = mesh.devices.shape
    chip_mesh = jax.sharding.Mesh(mesh.devices.reshape(groups, lanes // 2, 2), ("dp", "chip", "core"))
    in_specs = (
        P("dp", TENSOR, None),
        P(),
        P(None, "dp"),
        P("dp", None),
        P("dp", TENSOR, None, None),
        P("dp", None),
        P(),
        P("dp", TENSOR, None),
        P("dp", TENSOR, None),
        P(TENSOR, None, None),
        P(TENSOR, None, None),
    )
    out_specs = (P("dp", TENSOR, None), P("dp", TENSOR, None))
    return jax.shard_map(shards, mesh=chip_mesh, in_specs=in_specs, out_specs=out_specs, check_vma=False)
```

```python
import jax
import jax.numpy as jnp
from jax import lax
from jax.sharding import PartitionSpec as P

HEADS = 24
KV_HEADS = 8
HEAD_DIM = 64
EXPERTS = 32
TOPK = 8
SHIFTS = 2
CAP = 40
TENSOR = ("chip", "core")


EPS = 1e-06
THETA = 10000.0


def from_behind(value, axis, steps):
    count = lax.axis_size(axis)
    first, last = (max(0, -steps), min(count, count - steps))
    return lax.ppermute(value, axis, [(source, source + steps) for source in range(first, last)])


def rms_norm(x, gain):
    values = x.astype(jnp.float32)
    mean_sq = jnp.mean(values * values, axis=-1, keepdims=True)
    return (values * lax.rsqrt(mean_sq + EPS) * gain).astype(jnp.bfloat16)


def rotary(x, positions):
    half = x.shape[-1] // 2
    freqs = THETA ** (-jnp.arange(half, dtype=jnp.float32) * 2.0 / x.shape[-1])
    angles = positions.astype(jnp.float32)[:, None] * freqs[None, :]
    cosine = jnp.concatenate([jnp.cos(angles), jnp.cos(angles)], axis=-1)[:, None, :]
    sine = jnp.concatenate([jnp.sin(angles), jnp.sin(angles)], axis=-1)[:, None, :]
    turned = jnp.concatenate([-x[..., half:], x[..., :half]], axis=-1)
    return x * cosine + turned * sine


def request_info(index, lengths):
    ends = jnp.cumsum(lengths, dtype=jnp.int32)
    before = ends[None, :] <= index[:, None]
    segment = jnp.sum(before.astype(jnp.int32), axis=1, dtype=jnp.int32)
    start = jnp.sum(jnp.where(before, lengths[None, :], 0), axis=1, dtype=jnp.int32)
    return (segment, index - start)


def merge_block(carry, scores, values, visible):
    best, total, acc = carry
    if visible is not None:
        scores = jnp.where(visible, scores, -1e30)
    newest = jnp.maximum(best, jnp.max(scores, axis=-1))
    probs = jnp.exp(scores - newest[..., None])
    if visible is not None:
        probs = jnp.where(visible, probs, 0.0)
    decay = jnp.exp(best - newest)
    total = total * decay + jnp.sum(probs, axis=-1)
    acc = acc * decay[..., None] + jnp.einsum(
        "tgrn,ngd->tgrd", probs.astype(jnp.bfloat16), values, preferred_element_type=jnp.float32
    )
    return (newest, total, acc)


def shards(
    tokens,
    attn_gain,
    qkv_weight,
    out_weight,
    prefix_cache,
    lengths,
    ffn_gain,
    expert_ids,
    gate_weights,
    expert_in,
    expert_out,
):
    rows = tokens.shape[1]
    model = tokens.shape[2]
    head_cols = HEADS * HEAD_DIM
    kv_cols = KV_HEADS * HEAD_DIM
    ratio = HEADS // KV_HEADS
    scale = 1.0 / HEAD_DIM**0.5
    lanes = lax.axis_size(TENSOR)
    prefix_len = prefix_cache.shape[1] * lanes
    own_lengths = lengths[0]
    inputs = tokens[0]
    normed = rms_norm(inputs, attn_gain)
    groups = lax.axis_size("dp")
    out_spread = jnp.broadcast_to(out_weight[None], (groups,) + out_weight.shape)
    full_out = lax.all_to_all(out_spread, "dp", 0, 0, tiled=True).reshape(groups * out_weight.shape[0], -1)
    spread = jnp.broadcast_to(normed[None], (groups, rows, model))
    group_rows = lax.all_to_all(spread, "dp", 0, 0, tiled=True).reshape(groups * rows, model)
    qkv_part = jnp.dot(group_rows, qkv_weight, preferred_element_type=jnp.float32).astype(jnp.bfloat16)
    qkv_back = lax.all_to_all(qkv_part.reshape(groups, rows, -1), "dp", 0, 0, tiled=True)
    qkv = jnp.transpose(qkv_back, (1, 0, 2)).reshape(rows, -1)
    lane = lax.axis_index(TENSOR)
    q_index = lane * rows + jnp.arange(rows, dtype=jnp.int32)
    q_segment, offset = request_info(q_index, own_lengths)
    positions = prefix_len + offset
    query = rotary(
        qkv[:, :head_cols].astype(jnp.float32).reshape(rows, HEADS, HEAD_DIM), positions
    ).astype(jnp.bfloat16)
    query = query.reshape(rows, KV_HEADS, ratio, HEAD_DIM)
    keys = rotary(
        qkv[:, head_cols : head_cols + kv_cols]
        .astype(jnp.float32)
        .reshape(rows, KV_HEADS, HEAD_DIM),
        positions,
    ).astype(jnp.bfloat16)
    local_pairs = jnp.stack([keys.reshape(rows, kv_cols), qkv[:, head_cols + kv_cols :]], axis=1)
    start_carry = (
        jnp.full((rows, KV_HEADS, ratio), -1e30, jnp.float32),
        jnp.zeros((rows, KV_HEADS, ratio), jnp.float32),
        jnp.zeros((rows, KV_HEADS, ratio, HEAD_DIM), jnp.float32),
    )
    window = local_pairs[None]
    for bit in range(SHIFTS):
        earlier = from_behind(window, TENSOR, 2**bit)
        window = jnp.concatenate([window, earlier], axis=0)
    depth = window.shape[0]
    k_index = (
        (lane - jnp.arange(depth, dtype=jnp.int32))[:, None] * rows
        + jnp.arange(rows, dtype=jnp.int32)[None, :]
    ).reshape(-1)
    k_segment, unused = request_info(k_index, own_lengths)
    visible = (
        (k_index[None, :] >= 0)
        & (k_index[None, :] <= q_index[:, None])
        & (k_segment[None, :] == q_segment[:, None])
    )
    suffix_pairs = window.reshape(depth * rows, 2, kv_cols)
    suffix_keys = suffix_pairs[:, 0].reshape(depth * rows, KV_HEADS, HEAD_DIM)
    suffix_values = suffix_pairs[:, 1].reshape(depth * rows, KV_HEADS, HEAD_DIM)
    scores = (
        jnp.einsum("tgrd,ngd->tgrn", query, suffix_keys, preferred_element_type=jnp.float32) * scale
    )
    carry = merge_block(start_carry, scores, suffix_values, visible[:, None, None, :])
    piece = lax.all_gather(prefix_cache[0], TENSOR, axis=0, tiled=True)
    piece, carry = lax.optimization_barrier((piece, carry))
    count = piece.shape[0]
    cached_keys = piece[:, 0].reshape(count, KV_HEADS, HEAD_DIM)
    cached_values = piece[:, 1].reshape(count, KV_HEADS, HEAD_DIM)
    scores = (
        jnp.einsum("tgrd,ngd->tgrn", query, cached_keys, preferred_element_type=jnp.float32) * scale
    )
    best, total, acc = merge_block(carry, scores, cached_values, None)
    attended = (acc / total[..., None]).astype(jnp.bfloat16).reshape(rows, head_cols)
    projected = jnp.dot(attended, full_out, preferred_element_type=jnp.float32)
    hidden_state = (inputs.astype(jnp.float32) + projected).astype(jnp.bfloat16)
    moe_input = rms_norm(hidden_state, ffn_gain)
    chips = lax.axis_size("chip")
    weights_in, weights_out, moe_input = lax.optimization_barrier((expert_in[0], expert_out[0], moe_input))
    other_in, other_out = lax.ppermute((weights_in, weights_out), "core", [(0, 1), (1, 0)])
    unit_ff = expert_in.shape[2] // 2
    own_ids = expert_ids[0]
    picks = (own_ids[:, :, None] == jnp.arange(EXPERTS, dtype=jnp.int32)[None, None, :]).astype(jnp.float32)
    named = jnp.sum(picks, axis=1)
    gates = jnp.sum(picks * gate_weights[0][:, :, None], axis=1)
    order = jnp.arange(rows, dtype=jnp.int32)
    below = (order[None, :] < order[:, None]).astype(jnp.bfloat16)
    earlier = jnp.dot(below, named.astype(jnp.bfloat16), preferred_element_type=jnp.float32)
    at_slot = earlier[:, :, None] == jnp.arange(CAP, dtype=jnp.float32)[None, None, :]
    routes = jnp.where(at_slot, named[:, :, None], 0.0).reshape(rows, chips * CAP)
    weights = jnp.where(at_slot, gates[:, :, None], 0.0).reshape(rows, chips * CAP)
    outgoing = jnp.dot(routes.astype(jnp.bfloat16).T, moe_input, preferred_element_type=jnp.float32)
    outgoing = outgoing.astype(jnp.bfloat16).reshape(chips, CAP, model)
    arrived = lax.all_to_all(outgoing, "chip", 0, 0, tiled=True)

    def unit(block, w_in, w_out):
        inner = jnp.dot(block.reshape(chips * CAP, model), w_in, preferred_element_type=jnp.float32)
        activated = (jax.nn.silu(inner[:, :unit_ff]) * inner[:, unit_ff:]).astype(jnp.bfloat16)
        produced = jnp.dot(activated, w_out, preferred_element_type=jnp.float32).astype(jnp.bfloat16)
        return produced.reshape(chips, CAP, model)

    own_part = unit(arrived, expert_in[0], expert_out[0])
    partner = unit(arrived, other_in, other_out)
    summed = (own_part.astype(jnp.float32) + partner.astype(jnp.float32)).astype(jnp.bfloat16)
    returned = lax.all_to_all(summed, "chip", 0, 0, tiled=True)
    returned = returned.reshape(chips * CAP, model)
    weights_hi = weights.astype(jnp.bfloat16)
    weights_lo = (weights - weights_hi.astype(jnp.float32)).astype(jnp.bfloat16)
    combined = jnp.dot(weights_hi, returned, preferred_element_type=jnp.float32) + jnp.dot(
        weights_lo, returned, preferred_element_type=jnp.float32
    )
    mixed = (hidden_state.astype(jnp.float32) + combined).astype(jnp.bfloat16)
    return (hidden_state[None], mixed[None])


def solution(mesh):
    groups, lanes = mesh.devices.shape
    chip_mesh = jax.sharding.Mesh(mesh.devices.reshape(groups, lanes // 2, 2), ("dp", "chip", "core"))
    in_specs = (
        P("dp", TENSOR, None),
        P(),
        P(None, "dp"),
        P("dp", None),
        P("dp", TENSOR, None, None),
        P("dp", None),
        P(),
        P("dp", TENSOR, None),
        P("dp", TENSOR, None),
        P(TENSOR, None, None),
        P(TENSOR, None, None),
    )
    out_specs = (P("dp", TENSOR, None), P("dp", TENSOR, None))
    return jax.shard_map(shards, mesh=chip_mesh, in_specs=in_specs, out_specs=out_specs, check_vma=False)
```

```python
import jax
import jax.numpy as jnp
from jax import lax
from jax.sharding import PartitionSpec as P

HEADS = 24
KV_HEADS = 8
HEAD_DIM = 64
EXPERTS = 32
TOPK = 8
SHIFTS = 2
CAP = 40
TENSOR = ("chip", "core")


EPS = 1e-06
THETA = 10000.0


def from_behind(value, axis, steps):
    count = lax.axis_size(axis)
    first, last = (max(0, -steps), min(count, count - steps))
    return lax.ppermute(value, axis, [(source, source + steps) for source in range(first, last)])


def rms_norm(x, gain):
    values = x.astype(jnp.float32)
    mean_sq = jnp.mean(values * values, axis=-1, keepdims=True)
    return (values * lax.rsqrt(mean_sq + EPS) * gain).astype(jnp.bfloat16)


def rotary(x, positions):
    half = x.shape[-1] // 2
    freqs = THETA ** (-jnp.arange(half, dtype=jnp.float32) * 2.0 / x.shape[-1])
    angles = positions.astype(jnp.float32)[:, None] * freqs[None, :]
    cosine = jnp.concatenate([jnp.cos(angles), jnp.cos(angles)], axis=-1)[:, None, :]
    sine = jnp.concatenate([jnp.sin(angles), jnp.sin(angles)], axis=-1)[:, None, :]
    turned = jnp.concatenate([-x[..., half:], x[..., :half]], axis=-1)
    return x * cosine + turned * sine


def request_info(index, lengths):
    ends = jnp.cumsum(lengths, dtype=jnp.int32)
    before = ends[None, :] <= index[:, None]
    segment = jnp.sum(before.astype(jnp.int32), axis=1, dtype=jnp.int32)
    start = jnp.sum(jnp.where(before, lengths[None, :], 0), axis=1, dtype=jnp.int32)
    return (segment, index - start)


def merge_block(carry, scores, values, visible):
    best, total, acc = carry
    if visible is not None:
        scores = jnp.where(visible, scores, -1e30)
    newest = jnp.maximum(best, jnp.max(scores, axis=-1))
    probs = jnp.exp(scores - newest[..., None])
    if visible is not None:
        probs = jnp.where(visible, probs, 0.0)
    decay = jnp.exp(best - newest)
    total = total * decay + jnp.sum(probs, axis=-1)
    acc = acc * decay[..., None] + jnp.einsum(
        "tgrn,ngd->tgrd", probs.astype(jnp.bfloat16), values, preferred_element_type=jnp.float32
    )
    return (newest, total, acc)


def shards(
    tokens,
    attn_gain,
    qkv_weight,
    out_weight,
    prefix_cache,
    lengths,
    ffn_gain,
    expert_ids,
    gate_weights,
    expert_in,
    expert_out,
):
    rows = tokens.shape[1]
    model = tokens.shape[2]
    head_cols = HEADS * HEAD_DIM
    kv_cols = KV_HEADS * HEAD_DIM
    ratio = HEADS // KV_HEADS
    scale = 1.0 / HEAD_DIM**0.5
    lanes = lax.axis_size(TENSOR)
    prefix_len = prefix_cache.shape[1] * lanes
    own_lengths = lengths[0]
    inputs = tokens[0]
    normed = rms_norm(inputs, attn_gain)
    groups = lax.axis_size("dp")
    out_spread = jnp.broadcast_to(out_weight[None], (groups,) + out_weight.shape)
    full_out = lax.all_to_all(out_spread, "dp", 0, 0, tiled=True).reshape(groups * out_weight.shape[0], -1)
    spread = jnp.broadcast_to(normed[None], (groups, rows, model))
    group_rows = lax.all_to_all(spread, "dp", 0, 0, tiled=True).reshape(groups * rows, model)
    qkv_part = jnp.dot(group_rows, qkv_weight, preferred_element_type=jnp.float32).astype(jnp.bfloat16)
    qkv_back = lax.all_to_all(qkv_part.reshape(groups, rows, -1), "dp", 0, 0, tiled=True)
    qkv = jnp.transpose(qkv_back, (1, 0, 2)).reshape(rows, -1)
    lane = lax.axis_index(TENSOR)
    q_index = lane * rows + jnp.arange(rows, dtype=jnp.int32)
    q_segment, offset = request_info(q_index, own_lengths)
    positions = prefix_len + offset
    query = rotary(
        qkv[:, :head_cols].astype(jnp.float32).reshape(rows, HEADS, HEAD_DIM), positions
    ).astype(jnp.bfloat16)
    query = query.reshape(rows, KV_HEADS, ratio, HEAD_DIM)
    keys = rotary(
        qkv[:, head_cols : head_cols + kv_cols]
        .astype(jnp.float32)
        .reshape(rows, KV_HEADS, HEAD_DIM),
        positions,
    ).astype(jnp.bfloat16)
    local_pairs = jnp.stack([keys.reshape(rows, kv_cols), qkv[:, head_cols + kv_cols :]], axis=1)
    start_carry = (
        jnp.full((rows, KV_HEADS, ratio), -1e30, jnp.float32),
        jnp.zeros((rows, KV_HEADS, ratio), jnp.float32),
        jnp.zeros((rows, KV_HEADS, ratio, HEAD_DIM), jnp.float32),
    )
    window = local_pairs[None]
    for bit in range(SHIFTS):
        earlier = from_behind(window, TENSOR, 2**bit)
        window = jnp.concatenate([window, earlier], axis=0)
    weights_in, weights_out, window = lax.optimization_barrier((expert_in[0], expert_out[0], window))
    other_in, other_out = lax.ppermute((weights_in, weights_out), "core", [(0, 1), (1, 0)])
    depth = window.shape[0]
    k_index = (
        (lane - jnp.arange(depth, dtype=jnp.int32))[:, None] * rows
        + jnp.arange(rows, dtype=jnp.int32)[None, :]
    ).reshape(-1)
    k_segment, unused = request_info(k_index, own_lengths)
    visible = (
        (k_index[None, :] >= 0)
        & (k_index[None, :] <= q_index[:, None])
        & (k_segment[None, :] == q_segment[:, None])
    )
    suffix_pairs = window.reshape(depth * rows, 2, kv_cols)
    suffix_keys = suffix_pairs[:, 0].reshape(depth * rows, KV_HEADS, HEAD_DIM)
    suffix_values = suffix_pairs[:, 1].reshape(depth * rows, KV_HEADS, HEAD_DIM)
    scores = (
        jnp.einsum("tgrd,ngd->tgrn", query, suffix_keys, preferred_element_type=jnp.float32) * scale
    )
    carry = merge_block(start_carry, scores, suffix_values, visible[:, None, None, :])
    piece = lax.all_gather(prefix_cache[0], TENSOR, axis=0, tiled=True)
    piece, carry = lax.optimization_barrier((piece, carry))
    count = piece.shape[0]
    cached_keys = piece[:, 0].reshape(count, KV_HEADS, HEAD_DIM)
    cached_values = piece[:, 1].reshape(count, KV_HEADS, HEAD_DIM)
    scores = (
        jnp.einsum("tgrd,ngd->tgrn", query, cached_keys, preferred_element_type=jnp.float32) * scale
    )
    best, total, acc = merge_block(carry, scores, cached_values, None)
    attended = (acc / total[..., None]).astype(jnp.bfloat16).reshape(rows, head_cols)
    projected = jnp.dot(attended, full_out, preferred_element_type=jnp.float32)
    hidden_state = (inputs.astype(jnp.float32) + projected).astype(jnp.bfloat16)
    moe_input = rms_norm(hidden_state, ffn_gain)
    chips = lax.axis_size("chip")
    unit_ff = expert_in.shape[2] // 2
    own_ids = expert_ids[0]
    picks = (own_ids[:, :, None] == jnp.arange(EXPERTS, dtype=jnp.int32)[None, None, :]).astype(jnp.float32)
    named = jnp.sum(picks, axis=1)
    gates = jnp.sum(picks * gate_weights[0][:, :, None], axis=1)
    order = jnp.arange(rows, dtype=jnp.int32)
    below = (order[None, :] < order[:, None]).astype(jnp.bfloat16)
    earlier = jnp.dot(below, named.astype(jnp.bfloat16), preferred_element_type=jnp.float32)
    at_slot = earlier[:, :, None] == jnp.arange(CAP, dtype=jnp.float32)[None, None, :]
    routes = jnp.where(at_slot, named[:, :, None], 0.0).reshape(rows, chips * CAP)
    weights = jnp.where(at_slot, gates[:, :, None], 0.0).reshape(rows, chips * CAP)
    outgoing = jnp.dot(routes.astype(jnp.bfloat16).T, moe_input, preferred_element_type=jnp.float32)
    outgoing = outgoing.astype(jnp.bfloat16).reshape(chips, CAP, model)
    arrived = lax.all_to_all(outgoing, "chip", 0, 0, tiled=True)

    def unit(block, w_in, w_out):
        inner = jnp.dot(block.reshape(chips * CAP, model), w_in, preferred_element_type=jnp.float32)
        activated = (jax.nn.silu(inner[:, :unit_ff]) * inner[:, unit_ff:]).astype(jnp.bfloat16)
        produced = jnp.dot(activated, w_out, preferred_element_type=jnp.float32).astype(jnp.bfloat16)
        return produced.reshape(chips, CAP, model)

    own_part = unit(arrived, expert_in[0], expert_out[0])
    partner = unit(arrived, other_in, other_out)
    summed = (own_part.astype(jnp.float32) + partner.astype(jnp.float32)).astype(jnp.bfloat16)
    returned = lax.all_to_all(summed, "chip", 0, 0, tiled=True)
    returned = returned.reshape(chips * CAP, model)
    weights_hi = weights.astype(jnp.bfloat16)
    weights_lo = (weights - weights_hi.astype(jnp.float32)).astype(jnp.bfloat16)
    combined = jnp.dot(weights_hi, returned, preferred_element_type=jnp.float32) + jnp.dot(
        weights_lo, returned, preferred_element_type=jnp.float32
    )
    mixed = (hidden_state.astype(jnp.float32) + combined).astype(jnp.bfloat16)
    return (hidden_state[None], mixed[None])


def solution(mesh):
    groups, lanes = mesh.devices.shape
    chip_mesh = jax.sharding.Mesh(mesh.devices.reshape(groups, lanes // 2, 2), ("dp", "chip", "core"))
    in_specs = (
        P("dp", TENSOR, None),
        P(),
        P(None, "dp"),
        P("dp", None),
        P("dp", TENSOR, None, None),
        P("dp", None),
        P(),
        P("dp", TENSOR, None),
        P("dp", TENSOR, None),
        P(TENSOR, None, None),
        P(TENSOR, None, None),
    )
    out_specs = (P("dp", TENSOR, None), P("dp", TENSOR, None))
    return jax.shard_map(shards, mesh=chip_mesh, in_specs=in_specs, out_specs=out_specs, check_vma=False)
```

```python
import jax
import jax.numpy as jnp
from jax import lax
from jax.sharding import PartitionSpec as P

HEADS = 24
KV_HEADS = 8
HEAD_DIM = 64
EXPERTS = 32
TOPK = 8
SHIFTS = 2
CAP = 40
TENSOR = ("chip", "core")


EPS = 1e-06
THETA = 10000.0


def from_behind(value, axis, steps):
    count = lax.axis_size(axis)
    first, last = (max(0, -steps), min(count, count - steps))
    return lax.ppermute(value, axis, [(source, source + steps) for source in range(first, last)])


def rms_norm(x, gain):
    values = x.astype(jnp.float32)
    mean_sq = jnp.mean(values * values, axis=-1, keepdims=True)
    return (values * lax.rsqrt(mean_sq + EPS) * gain).astype(jnp.bfloat16)


def rotary(x, positions):
    half = x.shape[-1] // 2
    freqs = THETA ** (-jnp.arange(half, dtype=jnp.float32) * 2.0 / x.shape[-1])
    angles = positions.astype(jnp.float32)[:, None] * freqs[None, :]
    cosine = jnp.concatenate([jnp.cos(angles), jnp.cos(angles)], axis=-1)[:, None, :]
    sine = jnp.concatenate([jnp.sin(angles), jnp.sin(angles)], axis=-1)[:, None, :]
    turned = jnp.concatenate([-x[..., half:], x[..., :half]], axis=-1)
    return x * cosine + turned * sine


def request_info(index, lengths):
    ends = jnp.cumsum(lengths, dtype=jnp.int32)
    before = ends[None, :] <= index[:, None]
    segment = jnp.sum(before.astype(jnp.int32), axis=1, dtype=jnp.int32)
    start = jnp.sum(jnp.where(before, lengths[None, :], 0), axis=1, dtype=jnp.int32)
    return (segment, index - start)


def merge_block(carry, scores, values, visible):
    best, total, acc = carry
    if visible is not None:
        scores = jnp.where(visible, scores, -1e30)
    newest = jnp.maximum(best, jnp.max(scores, axis=-1))
    probs = jnp.exp(scores - newest[..., None])
    if visible is not None:
        probs = jnp.where(visible, probs, 0.0)
    decay = jnp.exp(best - newest)
    total = total * decay + jnp.sum(probs, axis=-1)
    acc = acc * decay[..., None] + jnp.einsum(
        "tgrn,ngd->tgrd", probs.astype(jnp.bfloat16), values, preferred_element_type=jnp.float32
    )
    return (newest, total, acc)


def shards(
    tokens,
    attn_gain,
    qkv_weight,
    out_weight,
    prefix_cache,
    lengths,
    ffn_gain,
    expert_ids,
    gate_weights,
    expert_in,
    expert_out,
):
    rows = tokens.shape[1]
    model = tokens.shape[2]
    head_cols = HEADS * HEAD_DIM
    kv_cols = KV_HEADS * HEAD_DIM
    ratio = HEADS // KV_HEADS
    scale = 1.0 / HEAD_DIM**0.5
    lanes = lax.axis_size(TENSOR)
    prefix_len = prefix_cache.shape[1] * lanes
    own_lengths = lengths[0]
    inputs = tokens[0]
    normed = rms_norm(inputs, attn_gain)
    groups = lax.axis_size("dp")
    out_spread = jnp.broadcast_to(out_weight[None], (groups,) + out_weight.shape)
    full_out = lax.all_to_all(out_spread, "dp", 0, 0, tiled=True).reshape(groups * out_weight.shape[0], -1)
    spread = jnp.broadcast_to(normed[None], (groups, rows, model))
    group_rows = lax.all_to_all(spread, "dp", 0, 0, tiled=True).reshape(groups * rows, model)
    qkv_part = jnp.dot(group_rows, qkv_weight, preferred_element_type=jnp.float32).astype(jnp.bfloat16)
    qkv_back = lax.all_to_all(qkv_part.reshape(groups, rows, -1), "dp", 0, 0, tiled=True)
    qkv = jnp.transpose(qkv_back, (1, 0, 2)).reshape(rows, -1)
    lane = lax.axis_index(TENSOR)
    q_index = lane * rows + jnp.arange(rows, dtype=jnp.int32)
    q_segment, offset = request_info(q_index, own_lengths)
    positions = prefix_len + offset
    query = rotary(
        qkv[:, :head_cols].astype(jnp.float32).reshape(rows, HEADS, HEAD_DIM), positions
    ).astype(jnp.bfloat16)
    query = query.reshape(rows, KV_HEADS, ratio, HEAD_DIM)
    keys = rotary(
        qkv[:, head_cols : head_cols + kv_cols]
        .astype(jnp.float32)
        .reshape(rows, KV_HEADS, HEAD_DIM),
        positions,
    ).astype(jnp.bfloat16)
    local_pairs = jnp.stack([keys.reshape(rows, kv_cols), qkv[:, head_cols + kv_cols :]], axis=1)
    start_carry = (
        jnp.full((rows, KV_HEADS, ratio), -1e30, jnp.float32),
        jnp.zeros((rows, KV_HEADS, ratio), jnp.float32),
        jnp.zeros((rows, KV_HEADS, ratio, HEAD_DIM), jnp.float32),
    )
    window = jnp.stack([local_pairs] + [from_behind(local_pairs, TENSOR, step) for step in range(1, 2**SHIFTS)])
    weights_in, weights_out, window = lax.optimization_barrier((expert_in[0], expert_out[0], window))
    other_in, other_out = lax.ppermute((weights_in, weights_out), "core", [(0, 1), (1, 0)])
    depth = window.shape[0]
    k_index = (
        (lane - jnp.arange(depth, dtype=jnp.int32))[:, None] * rows
        + jnp.arange(rows, dtype=jnp.int32)[None, :]
    ).reshape(-1)
    k_segment, unused = request_info(k_index, own_lengths)
    visible = (
        (k_index[None, :] >= 0)
        & (k_index[None, :] <= q_index[:, None])
        & (k_segment[None, :] == q_segment[:, None])
    )
    suffix_pairs = window.reshape(depth * rows, 2, kv_cols)
    suffix_keys = suffix_pairs[:, 0].reshape(depth * rows, KV_HEADS, HEAD_DIM)
    suffix_values = suffix_pairs[:, 1].reshape(depth * rows, KV_HEADS, HEAD_DIM)
    scores = (
        jnp.einsum("tgrd,ngd->tgrn", query, suffix_keys, preferred_element_type=jnp.float32) * scale
    )
    carry = merge_block(start_carry, scores, suffix_values, visible[:, None, None, :])
    piece = lax.all_gather(prefix_cache[0], TENSOR, axis=0, tiled=True)
    piece, carry = lax.optimization_barrier((piece, carry))
    count = piece.shape[0]
    cached_keys = piece[:, 0].reshape(count, KV_HEADS, HEAD_DIM)
    cached_values = piece[:, 1].reshape(count, KV_HEADS, HEAD_DIM)
    scores = (
        jnp.einsum("tgrd,ngd->tgrn", query, cached_keys, preferred_element_type=jnp.float32) * scale
    )
    best, total, acc = merge_block(carry, scores, cached_values, None)
    attended = (acc / total[..., None]).astype(jnp.bfloat16).reshape(rows, head_cols)
    projected = jnp.dot(attended, full_out, preferred_element_type=jnp.float32)
    hidden_state = (inputs.astype(jnp.float32) + projected).astype(jnp.bfloat16)
    moe_input = rms_norm(hidden_state, ffn_gain)
    chips = lax.axis_size("chip")
    unit_ff = expert_in.shape[2] // 2
    own_ids = expert_ids[0]
    picks = (own_ids[:, :, None] == jnp.arange(EXPERTS, dtype=jnp.int32)[None, None, :]).astype(jnp.float32)
    named = jnp.sum(picks, axis=1)
    gates = jnp.sum(picks * gate_weights[0][:, :, None], axis=1)
    order = jnp.arange(rows, dtype=jnp.int32)
    below = (order[None, :] < order[:, None]).astype(jnp.bfloat16)
    earlier = jnp.dot(below, named.astype(jnp.bfloat16), preferred_element_type=jnp.float32)
    at_slot = earlier[:, :, None] == jnp.arange(CAP, dtype=jnp.float32)[None, None, :]
    routes = jnp.where(at_slot, named[:, :, None], 0.0).reshape(rows, chips * CAP)
    weights = jnp.where(at_slot, gates[:, :, None], 0.0).reshape(rows, chips * CAP)
    outgoing = jnp.dot(routes.astype(jnp.bfloat16).T, moe_input, preferred_element_type=jnp.float32)
    outgoing = outgoing.astype(jnp.bfloat16).reshape(chips, CAP, model)
    arrived = lax.all_to_all(outgoing, "chip", 0, 0, tiled=True)

    def unit(block, w_in, w_out):
        inner = jnp.dot(block.reshape(chips * CAP, model), w_in, preferred_element_type=jnp.float32)
        activated = (jax.nn.silu(inner[:, :unit_ff]) * inner[:, unit_ff:]).astype(jnp.bfloat16)
        produced = jnp.dot(activated, w_out, preferred_element_type=jnp.float32).astype(jnp.bfloat16)
        return produced.reshape(chips, CAP, model)

    own_part = unit(arrived, expert_in[0], expert_out[0])
    partner = unit(arrived, other_in, other_out)
    summed = (own_part.astype(jnp.float32) + partner.astype(jnp.float32)).astype(jnp.bfloat16)
    returned = lax.all_to_all(summed, "chip", 0, 0, tiled=True)
    returned = returned.reshape(chips * CAP, model)
    weights_hi = weights.astype(jnp.bfloat16)
    weights_lo = (weights - weights_hi.astype(jnp.float32)).astype(jnp.bfloat16)
    combined = jnp.dot(weights_hi, returned, preferred_element_type=jnp.float32) + jnp.dot(
        weights_lo, returned, preferred_element_type=jnp.float32
    )
    mixed = (hidden_state.astype(jnp.float32) + combined).astype(jnp.bfloat16)
    return (hidden_state[None], mixed[None])


def solution(mesh):
    groups, lanes = mesh.devices.shape
    chip_mesh = jax.sharding.Mesh(mesh.devices.reshape(groups, lanes // 2, 2), ("dp", "chip", "core"))
    in_specs = (
        P("dp", TENSOR, None),
        P(),
        P(None, "dp"),
        P("dp", None),
        P("dp", TENSOR, None, None),
        P("dp", None),
        P(),
        P("dp", TENSOR, None),
        P("dp", TENSOR, None),
        P(TENSOR, None, None),
        P(TENSOR, None, None),
    )
    out_specs = (P("dp", TENSOR, None), P("dp", TENSOR, None))
    return jax.shard_map(shards, mesh=chip_mesh, in_specs=in_specs, out_specs=out_specs, check_vma=False)
```

```python
import jax
import jax.numpy as jnp
from jax import lax
from jax.sharding import PartitionSpec as P

HEADS = 24
KV_HEADS = 8
HEAD_DIM = 64
EXPERTS = 32
TOPK = 8
SHIFTS = 2
CAP = 40
TENSOR = ("chip", "core")


EPS = 1e-06
THETA = 10000.0


def from_behind(value, axis, steps):
    count = lax.axis_size(axis)
    first, last = (max(0, -steps), min(count, count - steps))
    return lax.ppermute(value, axis, [(source, source + steps) for source in range(first, last)])


def rms_norm(x, gain):
    values = x.astype(jnp.float32)
    mean_sq = jnp.mean(values * values, axis=-1, keepdims=True)
    return (values * lax.rsqrt(mean_sq + EPS) * gain).astype(jnp.bfloat16)


def rotary(x, positions):
    half = x.shape[-1] // 2
    freqs = THETA ** (-jnp.arange(half, dtype=jnp.float32) * 2.0 / x.shape[-1])
    angles = positions.astype(jnp.float32)[:, None] * freqs[None, :]
    cosine = jnp.concatenate([jnp.cos(angles), jnp.cos(angles)], axis=-1)[:, None, :]
    sine = jnp.concatenate([jnp.sin(angles), jnp.sin(angles)], axis=-1)[:, None, :]
    turned = jnp.concatenate([-x[..., half:], x[..., :half]], axis=-1)
    return x * cosine + turned * sine


def request_info(index, lengths):
    ends = jnp.cumsum(lengths, dtype=jnp.int32)
    before = ends[None, :] <= index[:, None]
    segment = jnp.sum(before.astype(jnp.int32), axis=1, dtype=jnp.int32)
    start = jnp.sum(jnp.where(before, lengths[None, :], 0), axis=1, dtype=jnp.int32)
    return (segment, index - start)


def merge_block(carry, scores, values, visible):
    best, total, acc = carry
    if visible is not None:
        scores = jnp.where(visible, scores, -1e30)
    newest = jnp.maximum(best, jnp.max(scores, axis=-1))
    probs = jnp.exp(scores - newest[..., None])
    if visible is not None:
        probs = jnp.where(visible, probs, 0.0)
    decay = jnp.exp(best - newest)
    total = total * decay + jnp.sum(probs, axis=-1)
    acc = acc * decay[..., None] + jnp.einsum(
        "tgrn,ngd->tgrd", probs.astype(jnp.bfloat16), values, preferred_element_type=jnp.float32
    )
    return (newest, total, acc)


def shards(
    tokens,
    attn_gain,
    qkv_weight,
    out_weight,
    prefix_cache,
    lengths,
    ffn_gain,
    expert_ids,
    gate_weights,
    expert_in,
    expert_out,
):
    rows = tokens.shape[1]
    model = tokens.shape[2]
    head_cols = HEADS * HEAD_DIM
    kv_cols = KV_HEADS * HEAD_DIM
    ratio = HEADS // KV_HEADS
    scale = 1.0 / HEAD_DIM**0.5
    lanes = lax.axis_size(TENSOR)
    prefix_len = prefix_cache.shape[1] * lanes
    own_lengths = lengths[0]
    inputs = tokens[0]
    normed = rms_norm(inputs, attn_gain)
    groups = lax.axis_size("dp")
    out_spread = jnp.broadcast_to(out_weight[None], (groups,) + out_weight.shape)
    full_out = lax.all_to_all(out_spread, "dp", 0, 0, tiled=True).reshape(groups * out_weight.shape[0], -1)
    spread = jnp.broadcast_to(normed[None], (groups, rows, model))
    group_rows = lax.all_to_all(spread, "dp", 0, 0, tiled=True).reshape(groups * rows, model)
    qkv_part = jnp.dot(group_rows, qkv_weight, preferred_element_type=jnp.float32).astype(jnp.bfloat16)
    qkv_back = lax.all_to_all(qkv_part.reshape(groups, rows, -1), "dp", 0, 0, tiled=True)
    qkv = jnp.transpose(qkv_back, (1, 0, 2)).reshape(rows, -1)
    lane = lax.axis_index(TENSOR)
    q_index = lane * rows + jnp.arange(rows, dtype=jnp.int32)
    q_segment, offset = request_info(q_index, own_lengths)
    positions = prefix_len + offset
    query = rotary(
        qkv[:, :head_cols].astype(jnp.float32).reshape(rows, HEADS, HEAD_DIM), positions
    ).astype(jnp.bfloat16)
    query = query.reshape(rows, KV_HEADS, ratio, HEAD_DIM)
    keys = rotary(
        qkv[:, head_cols : head_cols + kv_cols]
        .astype(jnp.float32)
        .reshape(rows, KV_HEADS, HEAD_DIM),
        positions,
    ).astype(jnp.bfloat16)
    local_pairs = jnp.stack([keys.reshape(rows, kv_cols), qkv[:, head_cols + kv_cols :]], axis=1)
    start_carry = (
        jnp.full((rows, KV_HEADS, ratio), -1e30, jnp.float32),
        jnp.zeros((rows, KV_HEADS, ratio), jnp.float32),
        jnp.zeros((rows, KV_HEADS, ratio, HEAD_DIM), jnp.float32),
    )
    window = jnp.stack([local_pairs] + [from_behind(local_pairs, TENSOR, step) for step in range(1, 2**SHIFTS)])
    weights_in, weights_out, window = lax.optimization_barrier((expert_in[0], expert_out[0], window))
    other_in, other_out = lax.ppermute((weights_in, weights_out), "core", [(0, 1), (1, 0)])
    depth = window.shape[0]
    k_index = (
        (lane - jnp.arange(depth, dtype=jnp.int32))[:, None] * rows
        + jnp.arange(rows, dtype=jnp.int32)[None, :]
    ).reshape(-1)
    k_segment, unused = request_info(k_index, own_lengths)
    visible = (
        (k_index[None, :] >= 0)
        & (k_index[None, :] <= q_index[:, None])
        & (k_segment[None, :] == q_segment[:, None])
    )
    suffix_pairs = window.reshape(depth * rows, 2, kv_cols)
    suffix_keys = suffix_pairs[:, 0].reshape(depth * rows, KV_HEADS, HEAD_DIM)
    suffix_values = suffix_pairs[:, 1].reshape(depth * rows, KV_HEADS, HEAD_DIM)
    scores = (
        jnp.einsum("tgrd,ngd->tgrn", query, suffix_keys, preferred_element_type=jnp.float32) * scale
    )
    carry = merge_block(start_carry, scores, suffix_values, visible[:, None, None, :])
    own_cache = prefix_cache[0]
    other_cache = lax.ppermute(own_cache, "core", [(0, 1), (1, 0)])
    low_core = lax.axis_index("core") == 0
    pair = jnp.where(
        low_core, jnp.concatenate([own_cache, other_cache], axis=0), jnp.concatenate([other_cache, own_cache], axis=0)
    )
    piece = lax.all_gather(pair, "chip", axis=0, tiled=True)
    piece, carry = lax.optimization_barrier((piece, carry))
    count = piece.shape[0]
    cached_keys = piece[:, 0].reshape(count, KV_HEADS, HEAD_DIM)
    cached_values = piece[:, 1].reshape(count, KV_HEADS, HEAD_DIM)
    scores = (
        jnp.einsum("tgrd,ngd->tgrn", query, cached_keys, preferred_element_type=jnp.float32) * scale
    )
    best, total, acc = merge_block(carry, scores, cached_values, None)
    attended = (acc / total[..., None]).astype(jnp.bfloat16).reshape(rows, head_cols)
    projected = jnp.dot(attended, full_out, preferred_element_type=jnp.float32)
    hidden_state = (inputs.astype(jnp.float32) + projected).astype(jnp.bfloat16)
    moe_input = rms_norm(hidden_state, ffn_gain)
    chips = lax.axis_size("chip")
    unit_ff = expert_in.shape[2] // 2
    own_ids = expert_ids[0]
    picks = (own_ids[:, :, None] == jnp.arange(EXPERTS, dtype=jnp.int32)[None, None, :]).astype(jnp.float32)
    named = jnp.sum(picks, axis=1)
    gates = jnp.sum(picks * gate_weights[0][:, :, None], axis=1)
    order = jnp.arange(rows, dtype=jnp.int32)
    below = (order[None, :] < order[:, None]).astype(jnp.bfloat16)
    earlier = jnp.dot(below, named.astype(jnp.bfloat16), preferred_element_type=jnp.float32)
    at_slot = earlier[:, :, None] == jnp.arange(CAP, dtype=jnp.float32)[None, None, :]
    routes = jnp.where(at_slot, named[:, :, None], 0.0).reshape(rows, chips * CAP)
    weights = jnp.where(at_slot, gates[:, :, None], 0.0).reshape(rows, chips * CAP)
    outgoing = jnp.dot(routes.astype(jnp.bfloat16).T, moe_input, preferred_element_type=jnp.float32)
    outgoing = outgoing.astype(jnp.bfloat16).reshape(chips, CAP, model)
    arrived = lax.all_to_all(outgoing, "chip", 0, 0, tiled=True)

    def unit(block, w_in, w_out):
        inner = jnp.dot(block.reshape(chips * CAP, model), w_in, preferred_element_type=jnp.float32)
        activated = (jax.nn.silu(inner[:, :unit_ff]) * inner[:, unit_ff:]).astype(jnp.bfloat16)
        produced = jnp.dot(activated, w_out, preferred_element_type=jnp.float32).astype(jnp.bfloat16)
        return produced.reshape(chips, CAP, model)

    own_part = unit(arrived, expert_in[0], expert_out[0])
    partner = unit(arrived, other_in, other_out)
    summed = (own_part.astype(jnp.float32) + partner.astype(jnp.float32)).astype(jnp.bfloat16)
    returned = lax.all_to_all(summed, "chip", 0, 0, tiled=True)
    returned = returned.reshape(chips * CAP, model)
    weights_hi = weights.astype(jnp.bfloat16)
    weights_lo = (weights - weights_hi.astype(jnp.float32)).astype(jnp.bfloat16)
    combined = jnp.dot(weights_hi, returned, preferred_element_type=jnp.float32) + jnp.dot(
        weights_lo, returned, preferred_element_type=jnp.float32
    )
    mixed = (hidden_state.astype(jnp.float32) + combined).astype(jnp.bfloat16)
    return (hidden_state[None], mixed[None])


def solution(mesh):
    groups, lanes = mesh.devices.shape
    chip_mesh = jax.sharding.Mesh(mesh.devices.reshape(groups, lanes // 2, 2), ("dp", "chip", "core"))
    in_specs = (
        P("dp", TENSOR, None),
        P(),
        P(None, "dp"),
        P("dp", None),
        P("dp", TENSOR, None, None),
        P("dp", None),
        P(),
        P("dp", TENSOR, None),
        P("dp", TENSOR, None),
        P(TENSOR, None, None),
        P(TENSOR, None, None),
    )
    out_specs = (P("dp", TENSOR, None), P("dp", TENSOR, None))
    return jax.shard_map(shards, mesh=chip_mesh, in_specs=in_specs, out_specs=out_specs, check_vma=False)
```

```python
import jax
import jax.numpy as jnp
from jax import lax
from jax.sharding import PartitionSpec as P

HEADS = 24
KV_HEADS = 8
HEAD_DIM = 64
EXPERTS = 32
TOPK = 8
SHIFTS = 2
CAP = 40
TENSOR = ("chip", "core")


EPS = 1e-06
THETA = 10000.0


def from_behind(value, axis, steps):
    count = lax.axis_size(axis)
    first, last = (max(0, -steps), min(count, count - steps))
    return lax.ppermute(value, axis, [(source, source + steps) for source in range(first, last)])


def rms_norm(x, gain):
    values = x.astype(jnp.float32)
    mean_sq = jnp.mean(values * values, axis=-1, keepdims=True)
    return (values * lax.rsqrt(mean_sq + EPS) * gain).astype(jnp.bfloat16)


def rotary(x, positions):
    half = x.shape[-1] // 2
    freqs = THETA ** (-jnp.arange(half, dtype=jnp.float32) * 2.0 / x.shape[-1])
    angles = positions.astype(jnp.float32)[:, None] * freqs[None, :]
    cosine = jnp.concatenate([jnp.cos(angles), jnp.cos(angles)], axis=-1)[:, None, :]
    sine = jnp.concatenate([jnp.sin(angles), jnp.sin(angles)], axis=-1)[:, None, :]
    turned = jnp.concatenate([-x[..., half:], x[..., :half]], axis=-1)
    return x * cosine + turned * sine


def request_info(index, lengths):
    ends = jnp.cumsum(lengths, dtype=jnp.int32)
    before = ends[None, :] <= index[:, None]
    segment = jnp.sum(before.astype(jnp.int32), axis=1, dtype=jnp.int32)
    start = jnp.sum(jnp.where(before, lengths[None, :], 0), axis=1, dtype=jnp.int32)
    return (segment, index - start)


def merge_block(carry, scores, values, visible):
    best, total, acc = carry
    if visible is not None:
        scores = jnp.where(visible, scores, -1e30)
    newest = jnp.maximum(best, jnp.max(scores, axis=-1))
    probs = jnp.exp(scores - newest[..., None])
    if visible is not None:
        probs = jnp.where(visible, probs, 0.0)
    decay = jnp.exp(best - newest)
    total = total * decay + jnp.sum(probs, axis=-1)
    acc = acc * decay[..., None] + jnp.einsum(
        "tgrn,ngd->tgrd", probs.astype(jnp.bfloat16), values, preferred_element_type=jnp.float32
    )
    return (newest, total, acc)


def shards(
    tokens,
    attn_gain,
    qkv_weight,
    out_weight,
    prefix_cache,
    lengths,
    ffn_gain,
    expert_ids,
    gate_weights,
    expert_in,
    expert_out,
):
    rows = tokens.shape[1]
    model = tokens.shape[2]
    head_cols = HEADS * HEAD_DIM
    kv_cols = KV_HEADS * HEAD_DIM
    ratio = HEADS // KV_HEADS
    scale = 1.0 / HEAD_DIM**0.5
    lanes = lax.axis_size(TENSOR)
    prefix_len = prefix_cache.shape[1] * lanes
    own_lengths = lengths[0]
    inputs = tokens[0]
    normed = rms_norm(inputs, attn_gain)
    groups = lax.axis_size("dp")
    out_spread = jnp.broadcast_to(out_weight[None], (groups,) + out_weight.shape)
    full_out = lax.all_to_all(out_spread, "dp", 0, 0, tiled=True).reshape(groups * out_weight.shape[0], -1)
    spread = jnp.broadcast_to(normed[None], (groups, rows, model))
    group_rows = lax.all_to_all(spread, "dp", 0, 0, tiled=True).reshape(groups * rows, model)
    qkv_part = jnp.dot(group_rows, qkv_weight, preferred_element_type=jnp.float32).astype(jnp.bfloat16)
    qkv_back = lax.all_to_all(qkv_part.reshape(groups, rows, -1), "dp", 0, 0, tiled=True)
    qkv = jnp.transpose(qkv_back, (1, 0, 2)).reshape(rows, -1)
    lane = lax.axis_index(TENSOR)
    q_index = lane * rows + jnp.arange(rows, dtype=jnp.int32)
    q_segment, offset = request_info(q_index, own_lengths)
    positions = prefix_len + offset
    query = rotary(
        qkv[:, :head_cols].astype(jnp.float32).reshape(rows, HEADS, HEAD_DIM), positions
    ).astype(jnp.bfloat16)
    query = query.reshape(rows, KV_HEADS, ratio, HEAD_DIM)
    keys = rotary(
        qkv[:, head_cols : head_cols + kv_cols]
        .astype(jnp.float32)
        .reshape(rows, KV_HEADS, HEAD_DIM),
        positions,
    ).astype(jnp.bfloat16)
    local_pairs = jnp.stack([keys.reshape(rows, kv_cols), qkv[:, head_cols + kv_cols :]], axis=1)
    start_carry = (
        jnp.full((rows, KV_HEADS, ratio), -1e30, jnp.float32),
        jnp.zeros((rows, KV_HEADS, ratio), jnp.float32),
        jnp.zeros((rows, KV_HEADS, ratio, HEAD_DIM), jnp.float32),
    )
    window = jnp.stack([local_pairs] + [from_behind(local_pairs, TENSOR, step) for step in range(1, 2**SHIFTS)])
    weights_in, weights_out, window = lax.optimization_barrier((expert_in[0], expert_out[0], window))
    other_in, other_out = lax.ppermute((weights_in, weights_out), "core", [(0, 1), (1, 0)])
    depth = window.shape[0]
    k_index = (
        (lane - jnp.arange(depth, dtype=jnp.int32))[:, None] * rows
        + jnp.arange(rows, dtype=jnp.int32)[None, :]
    ).reshape(-1)
    k_segment, unused = request_info(k_index, own_lengths)
    visible = (
        (k_index[None, :] >= 0)
        & (k_index[None, :] <= q_index[:, None])
        & (k_segment[None, :] == q_segment[:, None])
    )
    suffix_pairs = window.reshape(depth * rows, 2, kv_cols)
    suffix_keys = suffix_pairs[:, 0].reshape(depth * rows, KV_HEADS, HEAD_DIM)
    suffix_values = suffix_pairs[:, 1].reshape(depth * rows, KV_HEADS, HEAD_DIM)
    scores = (
        jnp.einsum("tgrd,ngd->tgrn", query, suffix_keys, preferred_element_type=jnp.float32) * scale
    )
    carry = merge_block(start_carry, scores, suffix_values, visible[:, None, None, :])
    piece = lax.all_gather(prefix_cache[0], TENSOR, axis=0, tiled=True)
    piece, carry = lax.optimization_barrier((piece, carry))
    count = piece.shape[0]
    cached_keys = piece[:, 0].reshape(count, KV_HEADS, HEAD_DIM)
    cached_values = piece[:, 1].reshape(count, KV_HEADS, HEAD_DIM)
    scores = (
        jnp.einsum("tgrd,ngd->tgrn", query, cached_keys, preferred_element_type=jnp.float32) * scale
    )
    best, total, acc = merge_block(carry, scores, cached_values, None)
    attended = (acc / total[..., None]).astype(jnp.bfloat16).reshape(rows, head_cols)
    projected = jnp.dot(attended, full_out, preferred_element_type=jnp.float32)
    hidden_state = (inputs.astype(jnp.float32) + projected).astype(jnp.bfloat16)
    moe_input = rms_norm(hidden_state, ffn_gain)
    chips = lax.axis_size("chip")
    unit_ff = expert_in.shape[2] // 2
    own_ids = expert_ids[0]
    picks = (own_ids[:, :, None] == jnp.arange(EXPERTS, dtype=jnp.int32)[None, None, :]).astype(jnp.float32)
    named = jnp.sum(picks, axis=1)
    gates = jnp.sum(picks * gate_weights[0][:, :, None], axis=1)
    order = jnp.arange(rows, dtype=jnp.int32)
    below = (order[None, :] < order[:, None]).astype(jnp.bfloat16)
    earlier = jnp.dot(below, named.astype(jnp.bfloat16), preferred_element_type=jnp.float32)
    at_slot = earlier[:, :, None] == jnp.arange(CAP, dtype=jnp.float32)[None, None, :]
    routes = jnp.where(at_slot, named[:, :, None], 0.0).reshape(rows, chips * CAP)
    weights = jnp.where(at_slot, gates[:, :, None], 0.0).reshape(rows, chips * CAP)
    outgoing = jnp.dot(routes.astype(jnp.bfloat16).T, moe_input, preferred_element_type=jnp.float32)
    outgoing = outgoing.astype(jnp.bfloat16).reshape(chips, CAP, model)
    arrived = lax.all_to_all(outgoing, "chip", 0, 0, tiled=True)

    def unit(block, w_in, w_out):
        inner = jnp.dot(block.reshape(chips * CAP, model), w_in, preferred_element_type=jnp.float32)
        activated = (jax.nn.silu(inner[:, :unit_ff]) * inner[:, unit_ff:]).astype(jnp.bfloat16)
        produced = jnp.dot(activated, w_out, preferred_element_type=jnp.float32).astype(jnp.bfloat16)
        return produced.reshape(chips, CAP, model)

    both_in = jnp.concatenate([expert_in[0], other_in], axis=1)
    inner_both = jnp.dot(arrived.reshape(chips * CAP, model), both_in, preferred_element_type=jnp.float32)
    width = expert_in.shape[2]

    def finish(inner, w_out):
        activated = (jax.nn.silu(inner[:, :unit_ff]) * inner[:, unit_ff:]).astype(jnp.bfloat16)
        produced = jnp.dot(activated, w_out, preferred_element_type=jnp.float32).astype(jnp.bfloat16)
        return produced.reshape(chips, CAP, model)

    own_part = finish(inner_both[:, :width], expert_out[0])
    partner = finish(inner_both[:, width:], other_out)
    summed = (own_part.astype(jnp.float32) + partner.astype(jnp.float32)).astype(jnp.bfloat16)
    returned = lax.all_to_all(summed, "chip", 0, 0, tiled=True)
    returned = returned.reshape(chips * CAP, model)
    weights_hi = weights.astype(jnp.bfloat16)
    weights_lo = (weights - weights_hi.astype(jnp.float32)).astype(jnp.bfloat16)
    combined = jnp.dot(weights_hi, returned, preferred_element_type=jnp.float32) + jnp.dot(
        weights_lo, returned, preferred_element_type=jnp.float32
    )
    mixed = (hidden_state.astype(jnp.float32) + combined).astype(jnp.bfloat16)
    return (hidden_state[None], mixed[None])


def solution(mesh):
    groups, lanes = mesh.devices.shape
    chip_mesh = jax.sharding.Mesh(mesh.devices.reshape(groups, lanes // 2, 2), ("dp", "chip", "core"))
    in_specs = (
        P("dp", TENSOR, None),
        P(),
        P(None, "dp"),
        P("dp", None),
        P("dp", TENSOR, None, None),
        P("dp", None),
        P(),
        P("dp", TENSOR, None),
        P("dp", TENSOR, None),
        P(TENSOR, None, None),
        P(TENSOR, None, None),
    )
    out_specs = (P("dp", TENSOR, None), P("dp", TENSOR, None))
    return jax.shard_map(shards, mesh=chip_mesh, in_specs=in_specs, out_specs=out_specs, check_vma=False)
```
